32 devices in a mesh: groups: 2 (over y), seq: 4 (over x, core), chan: 4 (over z).
Axes of the slice: x: 2, y: 2, z: 4, core: 2. Of those that a mesh axis runs over, the one named last changes fastest.
Arguments:
- tokens: bfloat16 [4096, 4096], P(('groups', 'seq'), 'chan'), parts along dimension 0, may hold values from -6 to 6
- norm_gain: float32 [4096], replicated, may hold values from 0.5 to 1.5
- proj_weight: bfloat16 [4096, 3, 4096], P('seq', None, 'chan'), may hold values from -0.09375 to 0.09375
- short_filter: float32 [3, 3, 4096], P(None, None, 'chan'), may hold values from -2.5 to 2.5
- long_filter: float32 [4096, 2048], P('chan', 'seq'), may hold values from -4 to 4, as said below
- skip_gain: float32 [4096], P('chan'), may hold values from 0.5 to 1.5
- out_weight: bfloat16 [4096, 4096], P(None, 'chan'), may hold values from -0.09375 to 0.09375
Outputs:
- block_out: bfloat16 [4096, 4096], P(('groups', 'seq'), 'chan'), parts along dimension 0
The draws below stay inside these ranges and needn't reach their ends.
There are 2 independent parts, one for each index of `groups`. The reference program is written for one: setup_inputs(seed, part) draws one part's arguments, and reference() takes and returns one part's arrays. A program takes and returns all parts, laid end to end along the dimension named above; an argument that names none is the same for every part. Nothing has to cross between parts.
Inputs may be any that keep to these rules, and one draw needn't show every extreme that they name: `long_filter`: filter taps of the sequence-long convolution.
All inputs are finite; a program needn't handle non-finite values.
Results may differ from the reference program's by a relative error of at most 0.012.
Values may be sent and summed in bfloat16 or wider, within the bound.
A program may use at most 128 MiB of HBM per device.

```python
import jax
import jax.numpy as jnp
from jax import lax

D = 4096
SHORT = 3
SEQ = 2048


def draw_long_filter(key, part):
    streams = jax.random.split(jax.random.fold_in(key, 17), 6)
    length = SEQ
    sequence_indices = jnp.arange(length, dtype=jnp.float32)
    fast_pick = jax.random.uniform(streams[0], (D,)) < 0.5
    fast_rate = jnp.exp(jax.random.uniform(streams[1], (D,), jnp.float32, jnp.log(1.0 / 50.0), jnp.log(1.0 / 30.0)))
    slow_rate = jnp.exp(jax.random.uniform(streams[2], (D,), jnp.float32, jnp.log(0.1 / length), jnp.log(2.0 / length)))
    attenuation_speeds = jnp.where(fast_pick, fast_rate, slow_rate)
    places = jax.random.randint(streams[3], (4,), 1, length)
    discarded_values = jax.random.uniform(streams[4], (D, 4), jnp.float32, 0.5, 0.8)
    successor_index = (sequence_indices[None, :] >= places[:, None].astype(jnp.float32)).astype(jnp.float32)
    sparse_impulse_list = jnp.exp(jnp.dot(jnp.log(discarded_values), successor_index))
    fading_profile = jnp.exp(-attenuation_speeds[:, None] * sequence_indices[None, :]) * sparse_impulse_list
    amplitude = lax.rsqrt(jnp.sum(fading_profile * fading_profile, axis=1))
    noise = jnp.clip(jax.random.normal(streams[5], (D, length), jnp.float32), -4.0, 4.0)
    return (noise * fading_profile * amplitude[:, None]).astype(jnp.float32)


def shard_levels(rng, shape, shards, smallest, high):
    gain = 1.0
    for axis_at, shards_of in shards:
        heights = jax.random.uniform(jax.random.fold_in(jax.random.fold_in(rng, 6), axis_at), (shards_of,), jnp.float32, smallest / len(shards), high / len(shards))
        gain = gain * jnp.repeat(jnp.exp(heights), shape[axis_at] // shards_of).reshape((-1,) + (1,) * (len(shape) - 1 - axis_at))
    return gain


def scatter_about(key, dims, deviation, limit, cuts=(), kind=jnp.bfloat16):
    factor_of = shard_levels(key, dims, cuts, -0.22, 0.18) if cuts else 1.0
    entries = jax.random.normal(key, dims, jnp.float32) * deviation * factor_of
    return jnp.minimum(jnp.maximum(entries, -limit), limit).astype(kind)


def setup_inputs(seed: int = 0, part: int = 0) -> dict:
    streams_of = jax.random.split(jax.random.key(seed), 8)
    own_keys = jax.random.split(jax.random.fold_in(streams_of[7], part), 8)
    return {
        "tokens": scatter_about(own_keys[0], (SEQ, D), 1.0, 6.0, ((0, 4), (1, 4))),
        "norm_gain": jnp.clip(1.0 + 0.1 * jax.random.normal(streams_of[1], (D,), jnp.float32), 0.5, 1.5),
        "proj_weight": scatter_about(streams_of[2], (D, 3, D), D ** -0.5, 0.09375, ((0, 4), (2, 4))),
        "short_filter": scatter_about(streams_of[3], (SHORT, 3, D), 0.6, 2.5, ((2, 4),), jnp.float32),
        "long_filter": draw_long_filter(jax.random.fold_in(streams_of[7], 71), part),
        "skip_gain": jnp.clip(0.5 + 1.0 * jax.random.uniform(streams_of[5], (D,), jnp.float32) ** shard_levels(streams_of[5], (D,), ((0, 4),), -0.2, 0.2), 0.5, 1.5),
        "out_weight": scatter_about(streams_of[6], (D, D), D ** -0.5, 0.09375, ((1, 4),)),
    }


def causal_conv(signal_rows, filter_rows):
    channels, length = signal_rows.shape
    padded_len = 2 * length
    block = 256

    def one_block(pair):
        sig_block, tap_block = pair
        spec_sig = jnp.fft.rfft(sig_block, n=padded_len, axis=1)
        spec_tap = jnp.fft.rfft(tap_block, n=padded_len, axis=1)
        return jnp.fft.irfft(spec_sig * spec_tap, n=padded_len, axis=1)[:, :length]
    outcome = lax.map(one_block, (signal_rows.reshape(channels // block, block, length), filter_rows.reshape(channels // block, block, filter_rows.shape[1])))
    return outcome.reshape(channels, length)

def reference(tokens, norm_gain, proj_weight, short_filter, long_filter, skip_gain, out_weight):
    wide = tokens.astype(jnp.float32)
    rescaled_signal = (wide * lax.rsqrt(lax.optimization_barrier(jnp.mean(wide * wide, axis=1, keepdims=True)) + 1e-06) * norm_gain).astype(jnp.bfloat16)
    projected = jnp.dot(rescaled_signal, proj_weight.reshape(D, 3 * D), preferred_element_type=jnp.float32)
    projected = projected.astype(jnp.bfloat16).reshape(SEQ, 3, D)
    padded = jnp.pad(projected.astype(jnp.float32), ((SHORT - 1, 0), (0, 0), (0, 0)))
    featured = jnp.zeros((SEQ, 3, D), jnp.float32)
    for tap in range(SHORT):
        featured = featured + short_filter[tap][None, :, :] * padded[SHORT - 1 - tap:SHORT - 1 - tap + SEQ]
    featured = featured.astype(jnp.bfloat16)
    branches = jnp.transpose(featured, (1, 2, 0))
    query = branches[0].astype(jnp.float32)
    keys_rows = branches[1].astype(jnp.float32)
    values_rows = branches[2].astype(jnp.float32)
    middle = keys_rows * values_rows
    longer = (causal_conv(middle, long_filter) + skip_gain[:, None] * middle).astype(jnp.bfloat16)
    gated = (query * longer.astype(jnp.float32)).astype(jnp.bfloat16)
    update = lax.dot_general(gated, out_weight, (((0,), (0,)), ((), ())), preferred_element_type=jnp.float32)
    return (wide + update).astype(jnp.bfloat16)
```

```python
import functools
import math

import jax
import jax.numpy as jnp
import numpy as np
from jax import lax
from jax.experimental import pallas as pl
from jax.experimental.pallas import tpu as pltpu
from jax.sharding import PartitionSpec as P

SHORT = 3


EPSILON = 1e-06
HIGHEST = lax.Precision.HIGHEST


def from_behind(value, axis, steps):
    count = lax.axis_size(axis)
    initial, last = (max(0, -steps), min(count, count - steps))
    return lax.ppermute(value, axis, [(source, source + steps) for source in range(initial, last)])


def angle_table(row_count, col_count, period, sign):
    row_index = lax.iota(jnp.int32, row_count)[:, None]
    col_index = lax.iota(jnp.int32, col_count)[None, :]
    angles = (row_index * col_index % period).astype(jnp.float32) * (sign * 2.0 * math.pi / period)
    return (jnp.cos(angles), jnp.sin(angles))


def forward_spectrum(signal_rows, first, second):
    channels = signal_rows.shape[0]
    grid_rows = signal_rows.reshape(channels, first, second)
    cos_first, sin_first = angle_table(first, first, first, -1.0)
    part_re = jnp.einsum("cab,ak->ckb", grid_rows, cos_first, precision=HIGHEST)
    part_im = jnp.einsum("cab,ak->ckb", grid_rows, sin_first, precision=HIGHEST)
    twist_cos, twist_sin = angle_table(first, second, first * second, -1.0)
    part_re, part_im = (
        part_re * twist_cos - part_im * twist_sin,
        part_re * twist_sin + part_im * twist_cos,
    )
    cos_second, sin_second = angle_table(second, second, second, -1.0)
    spectrum_real = jnp.einsum("ckb,bm->ckm", part_re, cos_second, precision=HIGHEST) - jnp.einsum(
        "ckb,bm->ckm", part_im, sin_second, precision=HIGHEST
    )
    spec_im = jnp.einsum("ckb,bm->ckm", part_re, sin_second, precision=HIGHEST) + jnp.einsum(
        "ckb,bm->ckm", part_im, cos_second, precision=HIGHEST
    )
    return (spectrum_real, spec_im)


def inverse_spectrum(spectrum_real, spec_im, first, second):
    channels = spectrum_real.shape[0]
    cos_second, sin_second = angle_table(second, second, second, 1.0)
    part_re = jnp.einsum("ckm,bm->ckb", spectrum_real, cos_second, precision=HIGHEST) - jnp.einsum(
        "ckm,bm->ckb", spec_im, sin_second, precision=HIGHEST
    )
    part_im = jnp.einsum("ckm,bm->ckb", spectrum_real, sin_second, precision=HIGHEST) + jnp.einsum(
        "ckm,bm->ckb", spec_im, cos_second, precision=HIGHEST
    )
    twist_cos, twist_sin = angle_table(first, second, first * second, 1.0)
    part_re, part_im = (
        part_re * twist_cos - part_im * twist_sin,
        part_re * twist_sin + part_im * twist_cos,
    )
    cos_first, sin_first = angle_table(first, first, first, 1.0)
    result = jnp.einsum("ckb,ak->cab", part_re, cos_first, precision=HIGHEST) - jnp.einsum(
        "ckb,ak->cab", part_im, sin_first, precision=HIGHEST
    )
    return result.reshape(channels, first * second) / (first * second)


def spectral_conv(signal_rows, filter_rows):
    channels, length = signal_rows.shape
    padded_len = 2 * length
    log_len = padded_len.bit_length() - 1
    first = 1 << log_len // 2
    second = padded_len // first
    zeros_tail = jnp.zeros((channels, length), jnp.float32)
    sig_re, sig_im = forward_spectrum(
        jnp.concatenate([signal_rows, zeros_tail], axis=1), first, second
    )
    tap_re, tap_im = forward_spectrum(
        jnp.concatenate([filter_rows, zeros_tail], axis=1), first, second
    )
    prod_re = sig_re * tap_re - sig_im * tap_im
    prod_im = sig_re * tap_im + sig_im * tap_re
    return inverse_spectrum(prod_re, prod_im, first, second)[:, :length]


def short_filter_output(projected, rim_cells, kernel_coefficients):
    count = kernel_coefficients.shape[0]
    steps_len = projected.shape[2]
    extended = jnp.concatenate([rim_cells, projected], axis=2).astype(jnp.float32)
    total = jnp.zeros(projected.shape, jnp.float32)
    for tap in range(count):
        total = (
            total
            + kernel_coefficients[tap][:, :, None]
            * extended[:, :, count - 1 - tap : count - 1 - tap + steps_len]
        )
    return total.astype(jnp.bfloat16)


def hyena_mixer(keys_rows, values_rows, long_taps, skip_part):
    middle = keys_rows.astype(jnp.float32) * values_rows.astype(jnp.float32)
    return (spectral_conv(middle, long_taps) + skip_part[:, None] * middle).astype(jnp.bfloat16)


def body(tokens, norm_gain, proj_weight, short_filter, long_filter, skip_gain, out_weight):
    seq_count = lax.axis_size("seq")
    local_rows = tokens.shape[0]
    local_chan = proj_weight.shape[2]
    subset = local_chan // seq_count
    length = local_rows * seq_count
    offset = lax.axis_index("seq") * subset
    whole = lax.all_gather(tokens, "chan", axis=1, tiled=True)
    wide = whole.astype(jnp.float32)
    rescaled_signal = (
        wide * lax.rsqrt(jnp.mean(wide * wide, axis=1, keepdims=True) + EPSILON) * norm_gain
    ).astype(jnp.bfloat16)
    projected = lax.dot_general(
        lax.all_gather(proj_weight, "seq", axis=0, tiled=True),
        rescaled_signal,
        (((0,), (1,)), ((), ())),
        preferred_element_type=jnp.float32,
    ).astype(jnp.bfloat16)
    taps_grid = long_filter.reshape(1, seq_count, subset, local_rows)
    long_taps = lax.all_to_all(taps_grid, "seq", split_axis=1, concat_axis=3, tiled=True).reshape(
        subset, length
    )
    skip_part = lax.dynamic_slice_in_dim(skip_gain, offset, subset, 0)
    rim_cells = from_behind(projected[:, :, local_rows - (SHORT - 1) :], "seq", 1)
    featured = short_filter_output(projected, rim_cells, short_filter)
    pair_grid = featured[1:].reshape(2, seq_count, subset, local_rows)
    moved = lax.all_to_all(pair_grid, "seq", split_axis=1, concat_axis=3, tiled=True).reshape(
        2, subset, length
    )
    result = hyena_mixer(moved[0], moved[1], long_taps, skip_part)
    returned = lax.all_to_all(
        result.reshape(1, subset, length), "seq", split_axis=2, concat_axis=0, tiled=True
    )
    returned = returned.reshape(local_chan, local_rows)
    gated = (featured[0].astype(jnp.float32) * returned.astype(jnp.float32)).astype(jnp.bfloat16)
    full_mix = lax.all_gather(gated, "chan", axis=0, tiled=True)
    update = lax.dot_general(
        full_mix, out_weight, (((0,), (0,)), ((), ())), preferred_element_type=jnp.float32
    )
    return (tokens.astype(jnp.float32) + update).astype(jnp.bfloat16)


TOKEN_CHUNKS = 8
WEIGHT_CHUNKS = 8
ANY = pl.BlockSpec(memory_space=pl.ANY)


def remote(src, dst, send_sem, recv_sem, where):
    return pltpu.make_async_remote_copy(
        src_ref=src,
        dst_ref=dst,
        send_sem=send_sem,
        recv_sem=recv_sem,
        device_id=where,
        device_id_type=pl.DeviceIdType.MESH,
    )


def greet(devices):
    barrier = pltpu.get_barrier_semaphore()
    for where, present in devices:

        @pl.when(present)
        def _():
            pl.semaphore_signal(
                barrier, inc=1, device_id=where, device_id_type=pl.DeviceIdType.MESH
            )

    pl.semaphore_wait(
        barrier, sum(jnp.asarray(present).astype(jnp.int32) for _, present in devices)
    )


class Line:
    def __init__(self, view, count, chunks, send_sem, recv_sem, place):
        self.view, self.count, self.chunks = view, count, chunks
        self.send_sem, self.recv_sem, self.place = send_sem, recv_sem, place
        self.me = lax.axis_index("chan")

    def copy(self, way, step, chunk, src=None):
        step_to = 1 if way == 0 else -1
        owner = jnp.clip(self.me - step * step_to, 0, self.count - 1)
        target = jnp.clip(self.me + step_to, 0, self.count - 1)
        block = self.view(owner, chunk)
        return remote(
            block if src is None else src,
            block,
            self.send_sem.at[way, step, chunk],
            self.recv_sem.at[way, step, chunk],
            self.place(target),
        )

    def sends(self, way, step):
        if way == 0:
            return (self.me - step >= 0) & (self.me + 1 < self.count)
        return (self.me + step < self.count) & (self.me - 1 >= 0)

    def receives(self, way, step):
        if way == 0:
            return self.me - 1 - step >= 0
        return self.me + 1 + step < self.count

    def arrived(self, way, step, chunk):
        step_to = 1 if way == 0 else -1
        owner = jnp.clip(self.me - (step + 1) * step_to, 0, self.count - 1)
        block = self.view(owner, chunk)
        remote(
            block,
            block,
            self.send_sem.at[way, step, chunk],
            self.recv_sem.at[way, step, chunk],
            self.place(self.me),
        ).wait_recv()
        return owner


def gather_inputs_kernel(
    sizes,
    tokens,
    weights,
    taps,
    all_tokens,
    all_weights,
    all_taps,
    token_room,
    weight_room,
    tap_room,
    local_sem,
    line_send,
    line_recv,
    mate_send,
    mate_recv,
    x_send,
    x_recv,
    y_send,
    y_recv,
    f_send,
    f_recv,
):
    chan_count = sizes
    y, s, z = (lax.axis_index(name) for name in ("groups", "seq", "chan"))
    x, core = s // 2, s % 2
    mate = (y, s + 1 - 2 * core, z)
    across = lambda to: (y, (1 - x) * 2 + to, z)
    beside = (1 - y, s, z)
    rows, width = tokens.shape
    depth = weights.shape[1]
    lags = taps.shape[2]
    half, half_lags = depth // 2, lags // 2

    greet(
        [
            (mate, True),
            (across(0), True),
            (across(1), True),
            (beside, True),
            ((y, s, jnp.minimum(z + 1, chan_count - 1)), z + 1 < chan_count),
            ((y, s, jnp.maximum(z - 1, 0)), z > 0),
        ]
    )

    token_rows = rows // TOKEN_CHUNKS
    weight_rows = half // WEIGHT_CHUNKS

    def token_view(owner, chunk):
        return all_tokens.at[
            pl.ds(core * rows + chunk * token_rows, token_rows), pl.ds(owner * width, width)
        ]

    line = Line(
        token_view, chan_count, TOKEN_CHUNKS, line_send, line_recv, lambda to: (y, s, to)
    )

    def weight_view(owner, part, chunk):
        return all_weights.at[pl.ds(owner * depth + part * half + chunk * weight_rows, weight_rows)]

    def tap_view(owner, part):
        return all_taps.at[pl.ds(owner * lags + part * half_lags, half_lags)]

    pending = []
    for chunk in range(TOKEN_CHUNKS):
        own = tokens.at[pl.ds(chunk * token_rows, token_rows)]
        for way in range(2):

            @pl.when(line.sends(way, 0))
            def _():
                line.copy(way, 0, chunk, own).start()

        for to in range(2):
            copy = remote(
                weights.at[to, pl.ds(y * half + chunk * weight_rows, weight_rows)],
                weight_view(s, y, chunk),
                x_send.at[to, chunk],
                x_recv.at[core, chunk],
                across(to),
            )
            copy.start()
            pending.append(copy)
    for to in range(2):
        copy = remote(
            taps.at[to, 1 - x, pl.ds(y * half_lags, half_lags)],
            tap_view(s, y),
            f_send.at[to],
            f_recv.at[core],
            across(to),
        )
        copy.start()
        pending.append(copy)
    own_view = all_tokens.at[pl.ds(core * rows, rows), pl.ds(z * width, width)]
    mate_copies = [
        remote(tokens, own_view, mate_send.at[0], mate_recv.at[0], mate),
        remote(
            weights.at[1 - core],
            all_weights.at[pl.ds(s * depth, depth)],
            mate_send.at[1],
            mate_recv.at[1],
            mate,
        ),
        remote(
            taps.at[1 - core, x],
            all_taps.at[pl.ds(s * lags, lags)],
            mate_send.at[2],
            mate_recv.at[2],
            mate,
        ),
    ]
    for copy in mate_copies:
        copy.start()
    ins = [
        pltpu.make_async_copy(tokens, token_room, local_sem.at[0]),
        pltpu.make_async_copy(weights.at[core], weight_room, local_sem.at[1]),
        pltpu.make_async_copy(taps.at[core, x], tap_room, local_sem.at[2]),
    ]
    outs = [
        pltpu.make_async_copy(token_room, own_view, local_sem.at[3]),
        pltpu.make_async_copy(
            weight_room, all_weights.at[pl.ds(s * depth, depth)], local_sem.at[4]
        ),
        pltpu.make_async_copy(tap_room, all_taps.at[pl.ds(s * lags, lags)], local_sem.at[5]),
    ]
    for copy in ins:
        copy.start()
    for first, second in zip(ins, outs):
        first.wait()
        second.start()

    def to_mate(way, step, chunk, owner):
        block = token_view(owner, chunk)
        index = 3 + (way * (chan_count - 1) + step) * TOKEN_CHUNKS + chunk
        return remote(block, block, mate_send.at[index], mate_recv.at[index], mate)

    steps = (chan_count - 1) * TOKEN_CHUNKS
    forwarded = 0
    for at in range(steps):
        step, chunk = divmod(at, TOKEN_CHUNKS)
        for way in range(2):

            @pl.when(line.receives(way, step))
            def _():
                owner = line.arrived(way, step, chunk)
                to_mate(way, step, chunk, owner).start()

            if step + 1 < chan_count - 1:

                @pl.when(line.receives(way, step) & line.sends(way, step + 1))
                def _():
                    line.copy(way, step + 1, chunk).start()

        while forwarded * steps < (at + 1) * WEIGHT_CHUNKS and forwarded < WEIGHT_CHUNKS:
            if (forwarded + 1) * steps > (at + 1) * WEIGHT_CHUNKS:
                break
            for origin in range(2):
                view = weight_view((1 - x) * 2 + origin, y, forwarded)
                remote(
                    view, view, x_send.at[origin, forwarded], x_recv.at[origin, forwarded], beside
                ).wait_recv()
                copy = remote(
                    view, view, y_send.at[origin, forwarded], y_recv.at[origin, forwarded], beside
                )
                copy.start()
                pending.append(copy)
            forwarded += 1
    for origin in range(2):
        view = tap_view((1 - x) * 2 + origin, y)
        remote(view, view, f_send.at[origin], f_recv.at[origin], beside).wait_recv()
        copy = remote(view, view, f_send.at[2 + origin], f_recv.at[2 + origin], beside)
        copy.start()
        pending.append(copy)

    for origin in range(2):
        owner = (1 - x) * 2 + origin
        for chunk in range(WEIGHT_CHUNKS):
            view = weight_view(owner, 1 - y, chunk)
            remote(
                view, view, y_send.at[origin, chunk], y_recv.at[origin, chunk], beside
            ).wait_recv()
        view = tap_view(owner, 1 - y)
        remote(view, view, f_send.at[2 + origin], f_recv.at[2 + origin], beside).wait_recv()
    for copy in outs:
        copy.wait()
    for copy in mate_copies:
        copy.wait_send()
    other_core = 1 - core
    mate_s = s + 1 - 2 * core
    for src, dst, index in (
        (tokens, all_tokens.at[pl.ds(other_core * rows, rows), pl.ds(z * width, width)], 0),
        (weights.at[0], all_weights.at[pl.ds(mate_s * depth, depth)], 1),
        (taps.at[0, 0], all_taps.at[pl.ds(mate_s * lags, lags)], 2),
    ):
        remote(src, dst, mate_send.at[index], mate_recv.at[index], mate).wait_recv()
    for at in range(steps):
        step, chunk = divmod(at, TOKEN_CHUNKS)
        for way in range(2):

            @pl.when(line.sends(way, step))
            def _():
                line.copy(way, step, chunk).wait_send()

            @pl.when(line.receives(way, step))
            def _():
                sign = 1 if way == 0 else -1
                owner = jnp.clip(z - (step + 1) * sign, 0, chan_count - 1)
                to_mate(way, step, chunk, owner).wait_send()
                block = all_tokens.at[
                    pl.ds(other_core * rows + chunk * token_rows, token_rows),
                    pl.ds(owner * width, width),
                ]
                index = 3 + (way * (chan_count - 1) + step) * TOKEN_CHUNKS + chunk
                remote(block, block, mate_send.at[index], mate_recv.at[index], mate).wait_recv()

    for copy in pending:
        copy.wait_send()


def gather_inputs(tokens, weights, taps, chan_count):
    rows, width = tokens.shape
    _, depth, columns = weights.shape
    lags, share = taps.shape[2:]
    mate_count = 3 + 2 * (chan_count - 1) * TOKEN_CHUNKS
    dma = pltpu.SemaphoreType.DMA
    return pl.pallas_call(
        functools.partial(gather_inputs_kernel, chan_count),
        out_shape=(
            jax.ShapeDtypeStruct((2 * rows, chan_count * width), tokens.dtype),
            jax.ShapeDtypeStruct((4 * depth, columns), weights.dtype),
            jax.ShapeDtypeStruct((4 * lags, share), taps.dtype),
        ),
        in_specs=[ANY] * 3,
        out_specs=[ANY] * 3,
        scratch_shapes=[
            pltpu.VMEM((rows, width), tokens.dtype),
            pltpu.VMEM((depth, columns), weights.dtype),
            pltpu.VMEM((lags, share), taps.dtype),
            dma((6,)),
            dma((2, chan_count - 1, TOKEN_CHUNKS)),
            dma((2, chan_count - 1, TOKEN_CHUNKS)),
            dma((mate_count,)),
            dma((mate_count,)),
            dma((2, WEIGHT_CHUNKS)),
            dma((2, WEIGHT_CHUNKS)),
            dma((2, WEIGHT_CHUNKS)),
            dma((2, WEIGHT_CHUNKS)),
            dma((4,)),
            dma((4,)),
        ],
        compiler_params=pltpu.CompilerParams(
            collective_id=0, has_side_effects=True
        ),
        name="gather_inputs",
    )(tokens, weights, taps)


def gather_gated_kernel(
    chan_count, gated, full, room, local_sem, mate_send, mate_recv, line_send, line_recv
):
    y, s, z = (lax.axis_index(name) for name in ("groups", "seq", "chan"))
    core = s % 2
    mate = (y, s + 1 - 2 * core, z)
    _, rows, width = gated.shape
    half_chunks = TOKEN_CHUNKS // 2
    chunk_rows = rows // half_chunks
    greet(
        [
            (mate, True),
            ((y, s, jnp.minimum(z + 1, chan_count - 1)), z + 1 < chan_count),
            ((y, s, jnp.maximum(z - 1, 0)), z > 0),
        ]
    )

    def view(owner, chunk):
        part, at = divmod(chunk, half_chunks)
        column = (owner * 2 + (core if part == 0 else 1 - core)) * width
        return full.at[pl.ds(at * chunk_rows, chunk_rows), pl.ds(column, width)]

    line = Line(view, chan_count, TOKEN_CHUNKS, line_send, line_recv, lambda to: (y, s, to))
    mine = (z * 2 + core) * width
    theirs = (z * 2 + 1 - core) * width
    swap = []
    for at in range(half_chunks):
        part = pl.ds(at * chunk_rows, chunk_rows)
        copy = remote(
            gated.at[1 - core, part],
            full.at[part, pl.ds(mine, width)],
            mate_send.at[at],
            mate_recv.at[at],
            mate,
        )
        copy.start()
        swap.append(copy)
    for chunk in range(half_chunks):
        own = gated.at[core, pl.ds(chunk * chunk_rows, chunk_rows)]
        for way in range(2):

            @pl.when(line.sends(way, 0))
            def _():
                line.copy(way, 0, chunk, own).start()

    take = pltpu.make_async_copy(gated.at[core], room, local_sem.at[0])
    take.start()
    for at in range(half_chunks):
        part = pl.ds(at * chunk_rows, chunk_rows)
        block = full.at[part, pl.ds(theirs, width)]
        remote(block, block, mate_send.at[at], mate_recv.at[at], mate).wait_recv()
        for way in range(2):

            @pl.when(line.sends(way, 0))
            def _():
                line.copy(way, 0, half_chunks + at).start()

    take.wait()
    put = pltpu.make_async_copy(room, full.at[:, pl.ds(mine, width)], local_sem.at[1])
    put.start()
    for step in range(chan_count - 1):
        for chunk in range(TOKEN_CHUNKS):
            for way in range(2):

                @pl.when(line.receives(way, step))
                def _():
                    line.arrived(way, step, chunk)

                if step + 1 < chan_count - 1:

                    @pl.when(line.receives(way, step) & line.sends(way, step + 1))
                    def _():
                        line.copy(way, step + 1, chunk).start()

    put.wait()
    for copy in swap:
        copy.wait_send()
    for step in range(chan_count - 1):
        for chunk in range(TOKEN_CHUNKS):
            for way in range(2):

                @pl.when(line.sends(way, step))
                def _():
                    line.copy(way, step, chunk).wait_send()


def gather_gated(gated, chan_count):
    _, rows, width = gated.shape
    dma = pltpu.SemaphoreType.DMA
    half_chunks = TOKEN_CHUNKS // 2
    return pl.pallas_call(
        functools.partial(gather_gated_kernel, chan_count),
        out_shape=jax.ShapeDtypeStruct((rows, 2 * chan_count * width), gated.dtype),
        in_specs=[ANY],
        out_specs=ANY,
        scratch_shapes=[
            pltpu.VMEM((rows, width), gated.dtype),
            dma((2,)),
            dma((half_chunks,)),
            dma((half_chunks,)),
            dma((2, chan_count - 1, TOKEN_CHUNKS)),
            dma((2, chan_count - 1, TOKEN_CHUNKS)),
        ],
        compiler_params=pltpu.CompilerParams(
            collective_id=1, has_side_effects=True
        ),
        name="gather_gated",
    )(gated)


def fourier_tables(length):
    points = 2 * length
    first = 1 << ((points.bit_length() - 1) // 2)
    second = points // first
    kept = first // 2 + 1
    padded = -(-2 * kept // 8) * 8
    low = np.arange(kept)
    place = second * np.arange(first // 2)[None, :] + np.arange(second)[:, None]
    angle = (low[None, :, None] * place[:, None, :] % points) * (2 * np.pi / points)
    outer = np.zeros((second, padded, first // 2))
    outer[:, :kept] = np.cos(angle)
    outer[:, kept : 2 * kept] = -np.sin(angle)
    gain = np.where((low == 0) | (low == first // 2), 1.0, 2.0)[None, None, :] / points
    back = np.zeros((second, first // 2, padded))
    back[:, :, :kept] = np.cos(angle).transpose(0, 2, 1) * gain
    back[:, :, kept : 2 * kept] = -np.sin(angle).transpose(0, 2, 1) * gain
    inner = (np.arange(second)[:, None] * np.arange(second)[None, :] % second) * (
        2 * np.pi / second
    )
    cos, sin = np.cos(inner), np.sin(inner)
    ahead = np.block([[cos, sin], [-sin, cos]])
    behind = np.block([[cos, -sin], [sin, cos]])
    return first, second, kept, padded, [
        jnp.asarray(table, jnp.bfloat16) for table in (outer, ahead, behind, back)
    ]


def long_conv_kernel(
    dims, signal, taps, skip, outer, ahead, behind, back, result, wide, spectra, total
):
    first, second, kept, padded = dims
    length, width = signal.shape
    reach = first // 2
    block = 64

    lanes = 128
    parts = width // lanes

    @pl.loop(0, length // block)
    def _(at):
        rows = pl.ds(pl.multiple_of(at * block, block), block)
        for part in range(parts):
            cols = pl.ds(part * lanes, lanes)
            wide[part, rows, :] = signal[rows, cols].astype(jnp.float32)
            wide[parts + part, rows, :] = taps[rows, cols].astype(jnp.float32)

    for part in range(parts):
        wide[parts + part, 0:1, :] = (
            wide[parts + part, 0:1, :] + skip[:, part * lanes : (part + 1) * lanes]
        )

    @pl.loop(0, second, unroll=2)
    def _(b):
        picked = jnp.concatenate(
            [wide.at[part][pl.ds(b, reach, stride=second), :] for part in range(2 * parts)],
            axis=1,
        ).astype(jnp.bfloat16)
        found = jnp.dot(outer[b], picked, preferred_element_type=jnp.float32)
        rows = pl.ds(pl.multiple_of(b * padded, 8), padded)
        for part in range(2 * parts):
            spectra[part, rows, :] = found[:, part * lanes : (part + 1) * lanes]

    def strided(start):
        return [
            spectra.at[part][pl.ds(start, second, stride=padded), :] for part in range(2 * parts)
        ]

    @pl.loop(0, kept)
    def _(k):
        real = jnp.concatenate(strided(k), axis=1)
        imag = jnp.concatenate(strided(k + kept), axis=1)
        both = jnp.concatenate([real, imag], axis=0).astype(jnp.bfloat16)
        freq = jnp.dot(ahead[...], both, preferred_element_type=jnp.float32)
        sr, si = freq[:second, :width], freq[second:, :width]
        hr, hi = freq[:second, width:], freq[second:, width:]
        product = jnp.concatenate([sr * hr - si * hi, sr * hi + si * hr], axis=0)
        inv = jnp.dot(
            behind[...], product.astype(jnp.bfloat16), preferred_element_type=jnp.float32
        )
        for part in range(parts):
            cols = slice(part * lanes, (part + 1) * lanes)
            spectra.at[part][pl.ds(k, second, stride=padded), :] = inv[:second, cols]
            spectra.at[part][pl.ds(k + kept, second, stride=padded), :] = inv[second:, cols]

    @pl.loop(0, second, unroll=2)
    def _(b):
        rows = pl.ds(pl.multiple_of(b * padded, 8), padded)
        filled = jnp.concatenate([spectra[part, rows, :] for part in range(parts)], axis=1)
        found = jnp.dot(back[b], filled.astype(jnp.bfloat16), preferred_element_type=jnp.float32)
        for part in range(parts):
            total.at[part][pl.ds(b, reach, stride=second), :] = found[
                :, part * lanes : (part + 1) * lanes
            ]

    @pl.loop(0, length // block)
    def _(at):
        rows = pl.ds(pl.multiple_of(at * block, block), block)
        for part in range(parts):
            result[rows, part * lanes : (part + 1) * lanes] = total[part, rows, :].astype(
                jnp.bfloat16
            )


def long_conv(signal, taps, skip):
    length, width = signal.shape
    first, second, kept, padded, tables = fourier_tables(length)
    return pl.pallas_call(
        functools.partial(long_conv_kernel, (first, second, kept, padded)),
        out_shape=jax.ShapeDtypeStruct((length, width), jnp.bfloat16),
        scratch_shapes=[
            pltpu.VMEM((2 * width // 128, length, 128), jnp.float32),
            pltpu.VMEM((2 * width // 128, second * padded, 128), jnp.float32),
            pltpu.VMEM((width // 128, length, 128), jnp.float32),
        ],
        compiler_params=pltpu.CompilerParams(vmem_limit_bytes=56 * 1024 * 1024),
        name="long_conv",
    )(signal, taps, skip, *tables)


def chip_body(tokens, norm_gain, proj_weight, short_filter, long_filter, skip_gain, out_weight):
    seq_count, chan_count = lax.axis_size("seq"), lax.axis_size("chan")
    rows, width = tokens.shape
    depth, branches, local_chan = proj_weight.shape
    half = local_chan // 2
    share = half // 2
    s = lax.axis_index("seq")
    x, core = s // 2, s % 2
    weights = (
        proj_weight.reshape(depth, branches, 2, half)
        .transpose(2, 0, 1, 3)
        .reshape(2, depth, branches * half)
    )
    taps = (
        long_filter.astype(jnp.bfloat16).reshape(2, 2, share, rows).transpose(0, 1, 3, 2)
    )
    whole, all_weights, all_taps = gather_inputs(tokens, weights, taps, chan_count)
    wide = whole.astype(jnp.float32)
    normed = (
        wide * lax.rsqrt(jnp.mean(wide * wide, axis=1, keepdims=True) + EPSILON) * norm_gain
    ).astype(jnp.bfloat16)
    projected = jnp.dot(normed, all_weights, preferred_element_type=jnp.float32).astype(
        jnp.bfloat16
    )
    rim = from_behind(projected[-(SHORT - 1) :], "seq", 2)
    short = lax.dynamic_slice_in_dim(short_filter, core * half, half, 2).reshape(
        SHORT, branches * half
    )
    extended = jnp.concatenate([rim, projected], axis=0).astype(jnp.float32)
    featured = jnp.zeros(projected.shape, jnp.float32)
    for tap in range(SHORT):
        start = SHORT - 1 - tap
        featured = featured + short[tap] * extended[start : start + projected.shape[0]]
    featured = featured.astype(jnp.bfloat16)
    middle = (
        featured[:, half : 2 * half].astype(jnp.float32)
        * featured[:, 2 * half :].astype(jnp.float32)
    ).astype(jnp.bfloat16)
    swap = [(at, (at + 2) % seq_count) for at in range(seq_count)]
    near = x == 0
    left, right = middle[:, :share], middle[:, share:]
    kept = jnp.where(near, left, right)
    other = lax.ppermute(jnp.where(near, right, left), "seq", swap)
    signal = jnp.concatenate(
        [jnp.where(near, kept, other), jnp.where(near, other, kept)], axis=0
    )
    skip = lax.dynamic_slice_in_dim(skip_gain, core * half + x * share, share, 0)
    longer = long_conv(signal, all_taps, skip[None, :])
    early, late = longer[: 2 * rows], longer[2 * rows :]
    kept = jnp.where(near, early, late)
    other = lax.ppermute(jnp.where(near, late, early), "seq", swap)
    longer = jnp.concatenate(
        [jnp.where(near, kept, other), jnp.where(near, other, kept)], axis=1
    )
    gated = (featured[:, :half].astype(jnp.float32) * longer.astype(jnp.float32)).astype(
        jnp.bfloat16
    )
    full_mix = gather_gated(gated.reshape(2, rows, half), chan_count)
    update = jnp.dot(full_mix, out_weight, preferred_element_type=jnp.float32)
    return (tokens.astype(jnp.float32) + update).astype(jnp.bfloat16)


def select_body(mesh):
    if mesh.shape["seq"] == 4 and mesh.shape["groups"] == 2:
        return chip_body
    return body


def solution(mesh):
    placed = (
        P(("groups", "seq"), "chan"),
        P(),
        P("seq", None, "chan"),
        P(None, None, "chan"),
        P("chan", "seq"),
        P("chan"),
        P(None, "chan"),
    )
    return jax.shard_map(
        select_body(mesh), mesh=mesh, in_specs=placed, out_specs=P(("groups", "seq"), "chan"), check_vma=False
    )
```

```python
import functools
import math

import jax
import jax.numpy as jnp
import numpy as np
from jax import lax
from jax.experimental import pallas as pl
from jax.experimental.pallas import tpu as pltpu
from jax.sharding import PartitionSpec as P

SHORT = 3


EPSILON = 1e-06
HIGHEST = lax.Precision.HIGHEST


def from_behind(value, axis, steps):
    count = lax.axis_size(axis)
    initial, last = (max(0, -steps), min(count, count - steps))
    return lax.ppermute(value, axis, [(source, source + steps) for source in range(initial, last)])


def angle_table(row_count, col_count, period, sign):
    row_index = lax.iota(jnp.int32, row_count)[:, None]
    col_index = lax.iota(jnp.int32, col_count)[None, :]
    angles = (row_index * col_index % period).astype(jnp.float32) * (sign * 2.0 * math.pi / period)
    return (jnp.cos(angles), jnp.sin(angles))


def forward_spectrum(signal_rows, first, second):
    channels = signal_rows.shape[0]
    grid_rows = signal_rows.reshape(channels, first, second)
    cos_first, sin_first = angle_table(first, first, first, -1.0)
    part_re = jnp.einsum("cab,ak->ckb", grid_rows, cos_first, precision=HIGHEST)
    part_im = jnp.einsum("cab,ak->ckb", grid_rows, sin_first, precision=HIGHEST)
    twist_cos, twist_sin = angle_table(first, second, first * second, -1.0)
    part_re, part_im = (
        part_re * twist_cos - part_im * twist_sin,
        part_re * twist_sin + part_im * twist_cos,
    )
    cos_second, sin_second = angle_table(second, second, second, -1.0)
    spectrum_real = jnp.einsum("ckb,bm->ckm", part_re, cos_second, precision=HIGHEST) - jnp.einsum(
        "ckb,bm->ckm", part_im, sin_second, precision=HIGHEST
    )
    spec_im = jnp.einsum("ckb,bm->ckm", part_re, sin_second, precision=HIGHEST) + jnp.einsum(
        "ckb,bm->ckm", part_im, cos_second, precision=HIGHEST
    )
    return (spectrum_real, spec_im)


def inverse_spectrum(spectrum_real, spec_im, first, second):
    channels = spectrum_real.shape[0]
    cos_second, sin_second = angle_table(second, second, second, 1.0)
    part_re = jnp.einsum("ckm,bm->ckb", spectrum_real, cos_second, precision=HIGHEST) - jnp.einsum(
        "ckm,bm->ckb", spec_im, sin_second, precision=HIGHEST
    )
    part_im = jnp.einsum("ckm,bm->ckb", spectrum_real, sin_second, precision=HIGHEST) + jnp.einsum(
        "ckm,bm->ckb", spec_im, cos_second, precision=HIGHEST
    )
    twist_cos, twist_sin = angle_table(first, second, first * second, 1.0)
    part_re, part_im = (
        part_re * twist_cos - part_im * twist_sin,
        part_re * twist_sin + part_im * twist_cos,
    )
    cos_first, sin_first = angle_table(first, first, first, 1.0)
    result = jnp.einsum("ckb,ak->cab", part_re, cos_first, precision=HIGHEST) - jnp.einsum(
        "ckb,ak->cab", part_im, sin_first, precision=HIGHEST
    )
    return result.reshape(channels, first * second) / (first * second)


def spectral_conv(signal_rows, filter_rows):
    channels, length = signal_rows.shape
    padded_len = 2 * length
    log_len = padded_len.bit_length() - 1
    first = 1 << log_len // 2
    second = padded_len // first
    zeros_tail = jnp.zeros((channels, length), jnp.float32)
    sig_re, sig_im = forward_spectrum(
        jnp.concatenate([signal_rows, zeros_tail], axis=1), first, second
    )
    tap_re, tap_im = forward_spectrum(
        jnp.concatenate([filter_rows, zeros_tail], axis=1), first, second
    )
    prod_re = sig_re * tap_re - sig_im * tap_im
    prod_im = sig_re * tap_im + sig_im * tap_re
    return inverse_spectrum(prod_re, prod_im, first, second)[:, :length]


def short_filter_output(projected, rim_cells, kernel_coefficients):
    count = kernel_coefficients.shape[0]
    steps_len = projected.shape[2]
    extended = jnp.concatenate([rim_cells, projected], axis=2).astype(jnp.float32)
    total = jnp.zeros(projected.shape, jnp.float32)
    for tap in range(count):
        total = (
            total
            + kernel_coefficients[tap][:, :, None]
            * extended[:, :, count - 1 - tap : count - 1 - tap + steps_len]
        )
    return total.astype(jnp.bfloat16)


def hyena_mixer(keys_rows, values_rows, long_taps, skip_part):
    middle = keys_rows.astype(jnp.float32) * values_rows.astype(jnp.float32)
    return (spectral_conv(middle, long_taps) + skip_part[:, None] * middle).astype(jnp.bfloat16)


def body(tokens, norm_gain, proj_weight, short_filter, long_filter, skip_gain, out_weight):
    seq_count = lax.axis_size("seq")
    local_rows = tokens.shape[0]
    local_chan = proj_weight.shape[2]
    subset = local_chan // seq_count
    length = local_rows * seq_count
    offset = lax.axis_index("seq") * subset
    whole = lax.all_gather(tokens, "chan", axis=1, tiled=True)
    wide = whole.astype(jnp.float32)
    rescaled_signal = (
        wide * lax.rsqrt(jnp.mean(wide * wide, axis=1, keepdims=True) + EPSILON) * norm_gain
    ).astype(jnp.bfloat16)
    projected = lax.dot_general(
        lax.all_gather(proj_weight, "seq", axis=0, tiled=True),
        rescaled_signal,
        (((0,), (1,)), ((), ())),
        preferred_element_type=jnp.float32,
    ).astype(jnp.bfloat16)
    taps_grid = long_filter.reshape(1, seq_count, subset, local_rows)
    long_taps = lax.all_to_all(taps_grid, "seq", split_axis=1, concat_axis=3, tiled=True).reshape(
        subset, length
    )
    skip_part = lax.dynamic_slice_in_dim(skip_gain, offset, subset, 0)
    rim_cells = from_behind(projected[:, :, local_rows - (SHORT - 1) :], "seq", 1)
    featured = short_filter_output(projected, rim_cells, short_filter)
    pair_grid = featured[1:].reshape(2, seq_count, subset, local_rows)
    moved = lax.all_to_all(pair_grid, "seq", split_axis=1, concat_axis=3, tiled=True).reshape(
        2, subset, length
    )
    result = hyena_mixer(moved[0], moved[1], long_taps, skip_part)
    returned = lax.all_to_all(
        result.reshape(1, subset, length), "seq", split_axis=2, concat_axis=0, tiled=True
    )
    returned = returned.reshape(local_chan, local_rows)
    gated = (featured[0].astype(jnp.float32) * returned.astype(jnp.float32)).astype(jnp.bfloat16)
    full_mix = lax.all_gather(gated, "chan", axis=0, tiled=True)
    update = lax.dot_general(
        full_mix, out_weight, (((0,), (0,)), ((), ())), preferred_element_type=jnp.float32
    )
    return (tokens.astype(jnp.float32) + update).astype(jnp.bfloat16)


TOKEN_CHUNKS = 8
WEIGHT_CHUNKS = 16
ANY = pl.BlockSpec(memory_space=pl.ANY)


def remote(src, dst, send_sem, recv_sem, where):
    return pltpu.make_async_remote_copy(
        src_ref=src,
        dst_ref=dst,
        send_sem=send_sem,
        recv_sem=recv_sem,
        device_id=where,
        device_id_type=pl.DeviceIdType.MESH,
    )


def greet(devices):
    barrier = pltpu.get_barrier_semaphore()
    for where, present in devices:

        @pl.when(present)
        def _():
            pl.semaphore_signal(
                barrier, inc=1, device_id=where, device_id_type=pl.DeviceIdType.MESH
            )

    pl.semaphore_wait(
        barrier, sum(jnp.asarray(present).astype(jnp.int32) for _, present in devices)
    )


class Line:
    def __init__(self, view, count, chunks, send_sem, recv_sem, place):
        self.view, self.count, self.chunks = view, count, chunks
        self.send_sem, self.recv_sem, self.place = send_sem, recv_sem, place
        self.me = lax.axis_index("chan")

    def copy(self, way, step, chunk, src=None):
        step_to = 1 if way == 0 else -1
        owner = jnp.clip(self.me - step * step_to, 0, self.count - 1)
        target = jnp.clip(self.me + step_to, 0, self.count - 1)
        block = self.view(owner, chunk)
        return remote(
            block if src is None else src,
            block,
            self.send_sem.at[way, step, chunk],
            self.recv_sem.at[way, step, chunk],
            self.place(target),
        )

    def sends(self, way, step):
        if way == 0:
            return (self.me - step >= 0) & (self.me + 1 < self.count)
        return (self.me + step < self.count) & (self.me - 1 >= 0)

    def receives(self, way, step):
        if way == 0:
            return self.me - 1 - step >= 0
        return self.me + 1 + step < self.count

    def arrived(self, way, step, chunk):
        step_to = 1 if way == 0 else -1
        owner = jnp.clip(self.me - (step + 1) * step_to, 0, self.count - 1)
        block = self.view(owner, chunk)
        remote(
            block,
            block,
            self.send_sem.at[way, step, chunk],
            self.recv_sem.at[way, step, chunk],
            self.place(self.me),
        ).wait_recv()
        return owner


def gather_inputs_kernel(
    sizes,
    tokens,
    weights,
    taps,
    all_tokens,
    all_weights,
    all_taps,
    token_room,
    weight_room,
    tap_room,
    local_sem,
    line_send,
    line_recv,
    mate_send,
    mate_recv,
    x_send,
    x_recv,
    y_send,
    y_recv,
    f_send,
    f_recv,
):
    chan_count = sizes
    y, s, z = (lax.axis_index(name) for name in ("groups", "seq", "chan"))
    x, core = s // 2, s % 2
    mate = (y, s + 1 - 2 * core, z)
    across = lambda to: (y, (1 - x) * 2 + to, z)
    beside = (1 - y, s, z)
    rows, width = tokens.shape
    branches, depth, columns = weights.shape[0], weights.shape[1], weights.shape[2] // 2
    lags = taps.shape[2]
    half, half_lags = depth // 2, lags // 2

    greet(
        [
            (mate, True),
            (across(0), True),
            (across(1), True),
            (beside, True),
            ((y, s, jnp.minimum(z + 1, chan_count - 1)), z + 1 < chan_count),
            ((y, s, jnp.maximum(z - 1, 0)), z > 0),
        ]
    )

    token_rows = rows // TOKEN_CHUNKS
    weight_rows = half // WEIGHT_CHUNKS

    def token_view(owner, chunk):
        return all_tokens.at[
            pl.ds(core * rows + chunk * token_rows, token_rows), pl.ds(owner * width, width)
        ]

    line = Line(
        token_view, chan_count, TOKEN_CHUNKS, line_send, line_recv, lambda to: (y, s, to)
    )

    def weight_view(owner, part, chunk):
        return all_weights.at[pl.ds(owner * depth + part * half + chunk * weight_rows, weight_rows)]

    def tap_view(owner, part):
        return all_taps.at[pl.ds(owner * lags + part * half_lags, half_lags)]

    pending = []
    for chunk in range(TOKEN_CHUNKS):
        own = tokens.at[pl.ds(chunk * token_rows, token_rows)]
        for way in range(2):

            @pl.when(line.sends(way, 0))
            def _():
                line.copy(way, 0, chunk, own).start()

    for chunk in range(WEIGHT_CHUNKS):
        for to in range(2):
            view = weight_view(s, y, chunk)
            for b in range(branches):
                remote(
                    weights.at[
                        b,
                        pl.ds(y * half + chunk * weight_rows, weight_rows),
                        pl.ds(to * columns, columns),
                    ],
                    view.at[:, pl.ds(b * columns, columns)],
                    x_send.at[to, chunk],
                    x_recv.at[core, chunk],
                    across(to),
                ).start()
            pending.append(
                remote(view, view, x_send.at[to, chunk], x_recv.at[core, chunk], across(to))
            )
    for to in range(2):
        copy = remote(
            taps.at[to, 1 - x, pl.ds(y * half_lags, half_lags)],
            tap_view(s, y),
            f_send.at[to],
            f_recv.at[core],
            across(to),
        )
        copy.start()
        pending.append(copy)
    own_view = all_tokens.at[pl.ds(core * rows, rows), pl.ds(z * width, width)]
    mate_copies = [
        remote(tokens, own_view, mate_send.at[0], mate_recv.at[0], mate),
        remote(
            all_weights.at[pl.ds(s * depth, depth)],
            all_weights.at[pl.ds(s * depth, depth)],
            mate_send.at[1],
            mate_recv.at[1],
            mate,
        ),
        remote(
            taps.at[1 - core, x],
            all_taps.at[pl.ds(s * lags, lags)],
            mate_send.at[2],
            mate_recv.at[2],
            mate,
        ),
    ]
    for copy in (mate_copies[0], mate_copies[2]):
        copy.start()
    for b in range(branches):
        remote(
            weights.at[b, :, pl.ds((1 - core) * columns, columns)],
            all_weights.at[pl.ds(s * depth, depth), pl.ds(b * columns, columns)],
            mate_send.at[1],
            mate_recv.at[1],
            mate,
        ).start()
    ins = [
        pltpu.make_async_copy(tokens, token_room, local_sem.at[0]),
        pltpu.make_async_copy(taps.at[core, x], tap_room, local_sem.at[1]),
    ] + [
        pltpu.make_async_copy(
            weights.at[b, :, pl.ds(core * columns, columns)],
            weight_room.at[:, pl.ds(b * columns, columns)],
            local_sem.at[2 + b],
        )
        for b in range(branches)
    ]
    outs = [
        pltpu.make_async_copy(token_room, own_view, local_sem.at[5]),
        pltpu.make_async_copy(tap_room, all_taps.at[pl.ds(s * lags, lags)], local_sem.at[6]),
    ] + [
        pltpu.make_async_copy(
            weight_room.at[:, pl.ds(b * columns, columns)],
            all_weights.at[pl.ds(s * depth, depth), pl.ds(b * columns, columns)],
            local_sem.at[7 + b],
        )
        for b in range(branches)
    ]
    for copy in ins:
        copy.start()
    for first, second in zip(ins, outs):
        first.wait()
        second.start()

    def to_mate(way, step, chunk, owner):
        block = token_view(owner, chunk)
        index = 3 + (way * (chan_count - 1) + step) * TOKEN_CHUNKS + chunk
        return remote(block, block, mate_send.at[index], mate_recv.at[index], mate)

    steps = (chan_count - 1) * TOKEN_CHUNKS
    forwarded = 0
    for at in range(steps):
        step, chunk = divmod(at, TOKEN_CHUNKS)
        for way in range(2):

            @pl.when(line.receives(way, step))
            def _():
                owner = line.arrived(way, step, chunk)
                to_mate(way, step, chunk, owner).start()

            if step + 1 < chan_count - 1:

                @pl.when(line.receives(way, step) & line.sends(way, step + 1))
                def _():
                    line.copy(way, step + 1, chunk).start()

        while forwarded * steps < (at + 1) * WEIGHT_CHUNKS and forwarded < WEIGHT_CHUNKS:
            if (forwarded + 1) * steps > (at + 1) * WEIGHT_CHUNKS:
                break
            for origin in range(2):
                view = weight_view((1 - x) * 2 + origin, y, forwarded)
                remote(
                    view, view, x_send.at[origin, forwarded], x_recv.at[origin, forwarded], beside
                ).wait_recv()
                copy = remote(
                    view, view, y_send.at[origin, forwarded], y_recv.at[origin, forwarded], beside
                )
                copy.start()
                pending.append(copy)
            forwarded += 1
    for origin in range(2):
        view = tap_view((1 - x) * 2 + origin, y)
        remote(view, view, f_send.at[origin], f_recv.at[origin], beside).wait_recv()
        copy = remote(view, view, f_send.at[2 + origin], f_recv.at[2 + origin], beside)
        copy.start()
        pending.append(copy)

    for origin in range(2):
        owner = (1 - x) * 2 + origin
        for chunk in range(WEIGHT_CHUNKS):
            view = weight_view(owner, 1 - y, chunk)
            remote(
                view, view, y_send.at[origin, chunk], y_recv.at[origin, chunk], beside
            ).wait_recv()
        view = tap_view(owner, 1 - y)
        remote(view, view, f_send.at[2 + origin], f_recv.at[2 + origin], beside).wait_recv()
    for copy in outs:
        copy.wait()
    for copy in mate_copies:
        copy.wait_send()
    other_core = 1 - core
    mate_s = s + 1 - 2 * core
    for src, dst, index in (
        (tokens, all_tokens.at[pl.ds(other_core * rows, rows), pl.ds(z * width, width)], 0),
        (
            all_weights.at[pl.ds(mate_s * depth, depth)],
            all_weights.at[pl.ds(mate_s * depth, depth)],
            1,
        ),
        (taps.at[0, 0], all_taps.at[pl.ds(mate_s * lags, lags)], 2),
    ):
        remote(src, dst, mate_send.at[index], mate_recv.at[index], mate).wait_recv()
    for at in range(steps):
        step, chunk = divmod(at, TOKEN_CHUNKS)
        for way in range(2):

            @pl.when(line.sends(way, step))
            def _():
                line.copy(way, step, chunk).wait_send()

            @pl.when(line.receives(way, step))
            def _():
                sign = 1 if way == 0 else -1
                owner = jnp.clip(z - (step + 1) * sign, 0, chan_count - 1)
                to_mate(way, step, chunk, owner).wait_send()
                block = all_tokens.at[
                    pl.ds(other_core * rows + chunk * token_rows, token_rows),
                    pl.ds(owner * width, width),
                ]
                index = 3 + (way * (chan_count - 1) + step) * TOKEN_CHUNKS + chunk
                remote(block, block, mate_send.at[index], mate_recv.at[index], mate).wait_recv()

    for copy in pending:
        copy.wait_send()


def gather_inputs(tokens, weights, taps, chan_count):
    rows, width = tokens.shape
    branches, depth, both = weights.shape
    columns = branches * both // 2
    lags, share = taps.shape[2:]
    mate_count = 3 + 2 * (chan_count - 1) * TOKEN_CHUNKS
    dma = pltpu.SemaphoreType.DMA
    return pl.pallas_call(
        functools.partial(gather_inputs_kernel, chan_count),
        out_shape=(
            jax.ShapeDtypeStruct((2 * rows, chan_count * width), tokens.dtype),
            jax.ShapeDtypeStruct((4 * depth, columns), weights.dtype),
            jax.ShapeDtypeStruct((4 * lags, share), taps.dtype),
        ),
        in_specs=[ANY] * 3,
        out_specs=[ANY] * 3,
        scratch_shapes=[
            pltpu.VMEM((rows, width), tokens.dtype),
            pltpu.VMEM((depth, columns), weights.dtype),
            pltpu.VMEM((lags, share), taps.dtype),
            dma((10,)),
            dma((2, chan_count - 1, TOKEN_CHUNKS)),
            dma((2, chan_count - 1, TOKEN_CHUNKS)),
            dma((mate_count,)),
            dma((mate_count,)),
            dma((2, WEIGHT_CHUNKS)),
            dma((2, WEIGHT_CHUNKS)),
            dma((2, WEIGHT_CHUNKS)),
            dma((2, WEIGHT_CHUNKS)),
            dma((4,)),
            dma((4,)),
        ],
        compiler_params=pltpu.CompilerParams(
            collective_id=0, has_side_effects=True
        ),
        name="gather_inputs",
    )(tokens, weights, taps)


def gather_gated_kernel(
    chan_count, gated, full, room, local_sem, mate_send, mate_recv, line_send, line_recv
):
    y, s, z = (lax.axis_index(name) for name in ("groups", "seq", "chan"))
    core = s % 2
    mate = (y, s + 1 - 2 * core, z)
    _, rows, width = gated.shape
    half_chunks = TOKEN_CHUNKS // 2
    chunk_rows = rows // half_chunks
    greet(
        [
            (mate, True),
            ((y, s, jnp.minimum(z + 1, chan_count - 1)), z + 1 < chan_count),
            ((y, s, jnp.maximum(z - 1, 0)), z > 0),
        ]
    )

    def view(owner, chunk):
        part, at = divmod(chunk, half_chunks)
        column = (owner * 2 + (core if part == 0 else 1 - core)) * width
        return full.at[pl.ds(at * chunk_rows, chunk_rows), pl.ds(column, width)]

    line = Line(view, chan_count, TOKEN_CHUNKS, line_send, line_recv, lambda to: (y, s, to))
    mine = (z * 2 + core) * width
    theirs = (z * 2 + 1 - core) * width
    swap = []
    for at in range(half_chunks):
        part = pl.ds(at * chunk_rows, chunk_rows)
        copy = remote(
            gated.at[1 - core, part],
            full.at[part, pl.ds(mine, width)],
            mate_send.at[at],
            mate_recv.at[at],
            mate,
        )
        copy.start()
        swap.append(copy)
    for chunk in range(half_chunks):
        own = gated.at[core, pl.ds(chunk * chunk_rows, chunk_rows)]
        for way in range(2):

            @pl.when(line.sends(way, 0))
            def _():
                line.copy(way, 0, chunk, own).start()

    take = pltpu.make_async_copy(gated.at[core], room, local_sem.at[0])
    take.start()
    for at in range(half_chunks):
        part = pl.ds(at * chunk_rows, chunk_rows)
        block = full.at[part, pl.ds(theirs, width)]
        remote(block, block, mate_send.at[at], mate_recv.at[at], mate).wait_recv()
        for way in range(2):

            @pl.when(line.sends(way, 0))
            def _():
                line.copy(way, 0, half_chunks + at).start()

    take.wait()
    put = pltpu.make_async_copy(room, full.at[:, pl.ds(mine, width)], local_sem.at[1])
    put.start()
    for step in range(chan_count - 1):
        for chunk in range(TOKEN_CHUNKS):
            for way in range(2):

                @pl.when(line.receives(way, step))
                def _():
                    line.arrived(way, step, chunk)

                if step + 1 < chan_count - 1:

                    @pl.when(line.receives(way, step) & line.sends(way, step + 1))
                    def _():
                        line.copy(way, step + 1, chunk).start()

    put.wait()
    for copy in swap:
        copy.wait_send()
    for step in range(chan_count - 1):
        for chunk in range(TOKEN_CHUNKS):
            for way in range(2):

                @pl.when(line.sends(way, step))
                def _():
                    line.copy(way, step, chunk).wait_send()


def gather_gated(gated, chan_count):
    _, rows, width = gated.shape
    dma = pltpu.SemaphoreType.DMA
    half_chunks = TOKEN_CHUNKS // 2
    return pl.pallas_call(
        functools.partial(gather_gated_kernel, chan_count),
        out_shape=jax.ShapeDtypeStruct((rows, 2 * chan_count * width), gated.dtype),
        in_specs=[ANY],
        out_specs=ANY,
        scratch_shapes=[
            pltpu.VMEM((rows, width), gated.dtype),
            dma((2,)),
            dma((half_chunks,)),
            dma((half_chunks,)),
            dma((2, chan_count - 1, TOKEN_CHUNKS)),
            dma((2, chan_count - 1, TOKEN_CHUNKS)),
        ],
        compiler_params=pltpu.CompilerParams(
            collective_id=1, has_side_effects=True
        ),
        name="gather_gated",
    )(gated)


def fourier_tables(length):
    points = 2 * length
    first = 1 << ((points.bit_length() - 1) // 2)
    second = points // first
    kept = first // 2 + 1
    padded = -(-2 * kept // 8) * 8
    low = np.arange(kept)
    place = second * np.arange(first // 2)[None, :] + np.arange(second)[:, None]
    angle = (low[None, :, None] * place[:, None, :] % points) * (2 * np.pi / points)
    outer = np.zeros((second, padded, first // 2))
    outer[:, :kept] = np.cos(angle)
    outer[:, kept : 2 * kept] = -np.sin(angle)
    gain = np.where((low == 0) | (low == first // 2), 1.0, 2.0)[None, None, :] / points
    back = np.zeros((second, first // 2, padded))
    back[:, :, :kept] = np.cos(angle).transpose(0, 2, 1) * gain
    back[:, :, kept : 2 * kept] = -np.sin(angle).transpose(0, 2, 1) * gain
    inner = (np.arange(second)[:, None] * np.arange(second)[None, :] % second) * (
        2 * np.pi / second
    )
    cos, sin = np.cos(inner), np.sin(inner)
    ahead = np.block([[cos, sin], [-sin, cos]])
    behind = np.block([[cos, -sin], [sin, cos]])
    return first, second, kept, padded, [
        jnp.asarray(table, jnp.bfloat16) for table in (outer, ahead, behind, back)
    ]


def long_conv_kernel(
    dims, signal, taps, skip, outer, ahead, behind, back, result, wide, spectra, total
):
    first, second, kept, padded = dims
    length, width = signal.shape
    reach = first // 2
    block = 64

    lanes = 128
    parts = width // lanes

    @pl.loop(0, length // block)
    def _(at):
        rows = pl.ds(pl.multiple_of(at * block, block), block)
        for part in range(parts):
            cols = pl.ds(part * lanes, lanes)
            wide[part, rows, :] = signal[rows, cols].astype(jnp.float32)
            wide[parts + part, rows, :] = taps[rows, cols].astype(jnp.float32)

    for part in range(parts):
        wide[parts + part, 0:1, :] = (
            wide[parts + part, 0:1, :] + skip[:, part * lanes : (part + 1) * lanes]
        )

    @pl.loop(0, second, unroll=4)
    def _(b):
        picked = jnp.concatenate(
            [wide.at[part][pl.ds(b, reach, stride=second), :] for part in range(2 * parts)],
            axis=1,
        ).astype(jnp.bfloat16)
        found = jnp.dot(outer[b], picked, preferred_element_type=jnp.float32)
        rows = pl.ds(pl.multiple_of(b * padded, 8), padded)
        for part in range(2 * parts):
            spectra[part, rows, :] = found[:, part * lanes : (part + 1) * lanes]

    def strided(start):
        return [
            spectra.at[part][pl.ds(start, second, stride=padded), :] for part in range(2 * parts)
        ]

    @pl.loop(0, kept, unroll=3)
    def _(k):
        real = jnp.concatenate(strided(k), axis=1)
        imag = jnp.concatenate(strided(k + kept), axis=1)
        both = jnp.concatenate([real, imag], axis=0).astype(jnp.bfloat16)
        freq = jnp.dot(ahead[...], both, preferred_element_type=jnp.float32)
        sr, si = freq[:second, :width], freq[second:, :width]
        hr, hi = freq[:second, width:], freq[second:, width:]
        product = jnp.concatenate([sr * hr - si * hi, sr * hi + si * hr], axis=0)
        inv = jnp.dot(
            behind[...], product.astype(jnp.bfloat16), preferred_element_type=jnp.float32
        )
        for part in range(parts):
            cols = slice(part * lanes, (part + 1) * lanes)
            spectra.at[part][pl.ds(k, second, stride=padded), :] = inv[:second, cols]
            spectra.at[part][pl.ds(k + kept, second, stride=padded), :] = inv[second:, cols]

    @pl.loop(0, second, unroll=4)
    def _(b):
        rows = pl.ds(pl.multiple_of(b * padded, 8), padded)
        filled = jnp.concatenate([spectra[part, rows, :] for part in range(parts)], axis=1)
        found = jnp.dot(back[b], filled.astype(jnp.bfloat16), preferred_element_type=jnp.float32)
        for part in range(parts):
            total.at[part][pl.ds(b, reach, stride=second), :] = found[
                :, part * lanes : (part + 1) * lanes
            ]

    @pl.loop(0, length // block)
    def _(at):
        rows = pl.ds(pl.multiple_of(at * block, block), block)
        for part in range(parts):
            result[rows, part * lanes : (part + 1) * lanes] = total[part, rows, :].astype(
                jnp.bfloat16
            )


def long_conv(signal, taps, skip):
    length, width = signal.shape
    first, second, kept, padded, tables = fourier_tables(length)
    return pl.pallas_call(
        functools.partial(long_conv_kernel, (first, second, kept, padded)),
        out_shape=jax.ShapeDtypeStruct((length, width), jnp.bfloat16),
        scratch_shapes=[
            pltpu.VMEM((2 * width // 128, length, 128), jnp.float32),
            pltpu.VMEM((2 * width // 128, second * padded, 128), jnp.float32),
            pltpu.VMEM((width // 128, length, 128), jnp.float32),
        ],
        compiler_params=pltpu.CompilerParams(vmem_limit_bytes=56 * 1024 * 1024),
        cost_estimate=pl.CostEstimate(
            flops=2 * 64 * length * width * 40, bytes_accessed=6 * length * width, transcendentals=0
        ),
        name="long_conv",
    )(signal, taps, skip, *tables)


def chip_body(tokens, norm_gain, proj_weight, short_filter, long_filter, skip_gain, out_weight):
    seq_count, chan_count = lax.axis_size("seq"), lax.axis_size("chan")
    rows, width = tokens.shape
    depth, branches, local_chan = proj_weight.shape
    half = local_chan // 2
    share = half // 2
    s = lax.axis_index("seq")
    x, core = s // 2, s % 2
    weights = proj_weight.transpose(1, 0, 2)
    taps = (
        long_filter.astype(jnp.bfloat16).reshape(2, 2, share, rows).transpose(0, 1, 3, 2)
    )
    whole, all_weights, all_taps = gather_inputs(tokens, weights, taps, chan_count)
    wide = whole.astype(jnp.float32)
    normed = (
        wide * lax.rsqrt(jnp.mean(wide * wide, axis=1, keepdims=True) + EPSILON) * norm_gain
    ).astype(jnp.bfloat16)
    projected = jnp.dot(normed, all_weights, preferred_element_type=jnp.float32).astype(
        jnp.bfloat16
    )
    rim = from_behind(projected[-(SHORT - 1) :], "seq", 2)
    short = lax.dynamic_slice_in_dim(short_filter, core * half, half, 2).reshape(
        SHORT, branches * half
    )
    extended = jnp.concatenate([rim, projected], axis=0).astype(jnp.float32)
    featured = jnp.zeros(projected.shape, jnp.float32)
    for tap in range(SHORT):
        start = SHORT - 1 - tap
        featured = featured + short[tap] * extended[start : start + projected.shape[0]]
    featured = featured.astype(jnp.bfloat16)
    middle = (
        featured[:, half : 2 * half].astype(jnp.float32)
        * featured[:, 2 * half :].astype(jnp.float32)
    ).astype(jnp.bfloat16)
    swap = [(at, (at + 2) % seq_count) for at in range(seq_count)]
    near = x == 0
    skip = lax.dynamic_slice_in_dim(skip_gain, core * half + x * share, share, 0)
    lanes = 128
    found = []
    for at in range(share // lanes):
        cols = slice(at * lanes, (at + 1) * lanes)
        left, right = middle[:, cols], middle[:, share:][:, cols]
        kept = jnp.where(near, left, right)
        other = lax.ppermute(jnp.where(near, right, left), "seq", swap)
        signal = jnp.concatenate(
            [jnp.where(near, kept, other), jnp.where(near, other, kept)], axis=0
        )
        longer = long_conv(signal, all_taps[:, cols], skip[None, cols])
        early, late = longer[: 2 * rows], longer[2 * rows :]
        kept = jnp.where(near, early, late)
        other = lax.ppermute(jnp.where(near, late, early), "seq", swap)
        found.append((jnp.where(near, kept, other), jnp.where(near, other, kept)))
    longer = jnp.concatenate([part[0] for part in found] + [part[1] for part in found], axis=1)
    gated = (featured[:, :half].astype(jnp.float32) * longer.astype(jnp.float32)).astype(
        jnp.bfloat16
    )
    full_mix = gather_gated(gated.reshape(2, rows, half), chan_count)
    update = jnp.dot(full_mix, out_weight, preferred_element_type=jnp.float32)
    return (tokens.astype(jnp.float32) + update).astype(jnp.bfloat16)


def select_body(mesh):
    if mesh.shape["seq"] == 4 and mesh.shape["groups"] == 2:
        return chip_body
    return body


def solution(mesh):
    placed = (
        P(("groups", "seq"), "chan"),
        P(),
        P("seq", None, "chan"),
        P(None, None, "chan"),
        P("chan", "seq"),
        P("chan"),
        P(None, "chan"),
    )
    return jax.shard_map(
        select_body(mesh), mesh=mesh, in_specs=placed, out_specs=P(("groups", "seq"), "chan"), check_vma=False
    )
```

```python
import functools
import math

import jax
import jax.numpy as jnp
import numpy as np
from jax import lax
from jax.experimental import pallas as pl
from jax.experimental.pallas import tpu as pltpu
from jax.sharding import PartitionSpec as P

SHORT = 3


EPSILON = 1e-06
HIGHEST = lax.Precision.HIGHEST


def from_behind(value, axis, steps):
    count = lax.axis_size(axis)
    initial, last = (max(0, -steps), min(count, count - steps))
    return lax.ppermute(value, axis, [(source, source + steps) for source in range(initial, last)])


def angle_table(row_count, col_count, period, sign):
    row_index = lax.iota(jnp.int32, row_count)[:, None]
    col_index = lax.iota(jnp.int32, col_count)[None, :]
    angles = (row_index * col_index % period).astype(jnp.float32) * (sign * 2.0 * math.pi / period)
    return (jnp.cos(angles), jnp.sin(angles))


def forward_spectrum(signal_rows, first, second):
    channels = signal_rows.shape[0]
    grid_rows = signal_rows.reshape(channels, first, second)
    cos_first, sin_first = angle_table(first, first, first, -1.0)
    part_re = jnp.einsum("cab,ak->ckb", grid_rows, cos_first, precision=HIGHEST)
    part_im = jnp.einsum("cab,ak->ckb", grid_rows, sin_first, precision=HIGHEST)
    twist_cos, twist_sin = angle_table(first, second, first * second, -1.0)
    part_re, part_im = (
        part_re * twist_cos - part_im * twist_sin,
        part_re * twist_sin + part_im * twist_cos,
    )
    cos_second, sin_second = angle_table(second, second, second, -1.0)
    spectrum_real = jnp.einsum("ckb,bm->ckm", part_re, cos_second, precision=HIGHEST) - jnp.einsum(
        "ckb,bm->ckm", part_im, sin_second, precision=HIGHEST
    )
    spec_im = jnp.einsum("ckb,bm->ckm", part_re, sin_second, precision=HIGHEST) + jnp.einsum(
        "ckb,bm->ckm", part_im, cos_second, precision=HIGHEST
    )
    return (spectrum_real, spec_im)


def inverse_spectrum(spectrum_real, spec_im, first, second):
    channels = spectrum_real.shape[0]
    cos_second, sin_second = angle_table(second, second, second, 1.0)
    part_re = jnp.einsum("ckm,bm->ckb", spectrum_real, cos_second, precision=HIGHEST) - jnp.einsum(
        "ckm,bm->ckb", spec_im, sin_second, precision=HIGHEST
    )
    part_im = jnp.einsum("ckm,bm->ckb", spectrum_real, sin_second, precision=HIGHEST) + jnp.einsum(
        "ckm,bm->ckb", spec_im, cos_second, precision=HIGHEST
    )
    twist_cos, twist_sin = angle_table(first, second, first * second, 1.0)
    part_re, part_im = (
        part_re * twist_cos - part_im * twist_sin,
        part_re * twist_sin + part_im * twist_cos,
    )
    cos_first, sin_first = angle_table(first, first, first, 1.0)
    result = jnp.einsum("ckb,ak->cab", part_re, cos_first, precision=HIGHEST) - jnp.einsum(
        "ckb,ak->cab", part_im, sin_first, precision=HIGHEST
    )
    return result.reshape(channels, first * second) / (first * second)


def spectral_conv(signal_rows, filter_rows):
    channels, length = signal_rows.shape
    padded_len = 2 * length
    log_len = padded_len.bit_length() - 1
    first = 1 << log_len // 2
    second = padded_len // first
    zeros_tail = jnp.zeros((channels, length), jnp.float32)
    sig_re, sig_im = forward_spectrum(
        jnp.concatenate([signal_rows, zeros_tail], axis=1), first, second
    )
    tap_re, tap_im = forward_spectrum(
        jnp.concatenate([filter_rows, zeros_tail], axis=1), first, second
    )
    prod_re = sig_re * tap_re - sig_im * tap_im
    prod_im = sig_re * tap_im + sig_im * tap_re
    return inverse_spectrum(prod_re, prod_im, first, second)[:, :length]


def short_filter_output(projected, rim_cells, kernel_coefficients):
    count = kernel_coefficients.shape[0]
    steps_len = projected.shape[2]
    extended = jnp.concatenate([rim_cells, projected], axis=2).astype(jnp.float32)
    total = jnp.zeros(projected.shape, jnp.float32)
    for tap in range(count):
        total = (
            total
            + kernel_coefficients[tap][:, :, None]
            * extended[:, :, count - 1 - tap : count - 1 - tap + steps_len]
        )
    return total.astype(jnp.bfloat16)


def hyena_mixer(keys_rows, values_rows, long_taps, skip_part):
    middle = keys_rows.astype(jnp.float32) * values_rows.astype(jnp.float32)
    return (spectral_conv(middle, long_taps) + skip_part[:, None] * middle).astype(jnp.bfloat16)


def body(tokens, norm_gain, proj_weight, short_filter, long_filter, skip_gain, out_weight):
    seq_count = lax.axis_size("seq")
    local_rows = tokens.shape[0]
    local_chan = proj_weight.shape[2]
    subset = local_chan // seq_count
    length = local_rows * seq_count
    offset = lax.axis_index("seq") * subset
    whole = lax.all_gather(tokens, "chan", axis=1, tiled=True)
    wide = whole.astype(jnp.float32)
    rescaled_signal = (
        wide * lax.rsqrt(jnp.mean(wide * wide, axis=1, keepdims=True) + EPSILON) * norm_gain
    ).astype(jnp.bfloat16)
    projected = lax.dot_general(
        lax.all_gather(proj_weight, "seq", axis=0, tiled=True),
        rescaled_signal,
        (((0,), (1,)), ((), ())),
        preferred_element_type=jnp.float32,
    ).astype(jnp.bfloat16)
    taps_grid = long_filter.reshape(1, seq_count, subset, local_rows)
    long_taps = lax.all_to_all(taps_grid, "seq", split_axis=1, concat_axis=3, tiled=True).reshape(
        subset, length
    )
    skip_part = lax.dynamic_slice_in_dim(skip_gain, offset, subset, 0)
    rim_cells = from_behind(projected[:, :, local_rows - (SHORT - 1) :], "seq", 1)
    featured = short_filter_output(projected, rim_cells, short_filter)
    pair_grid = featured[1:].reshape(2, seq_count, subset, local_rows)
    moved = lax.all_to_all(pair_grid, "seq", split_axis=1, concat_axis=3, tiled=True).reshape(
        2, subset, length
    )
    result = hyena_mixer(moved[0], moved[1], long_taps, skip_part)
    returned = lax.all_to_all(
        result.reshape(1, subset, length), "seq", split_axis=2, concat_axis=0, tiled=True
    )
    returned = returned.reshape(local_chan, local_rows)
    gated = (featured[0].astype(jnp.float32) * returned.astype(jnp.float32)).astype(jnp.bfloat16)
    full_mix = lax.all_gather(gated, "chan", axis=0, tiled=True)
    update = lax.dot_general(
        full_mix, out_weight, (((0,), (0,)), ((), ())), preferred_element_type=jnp.float32
    )
    return (tokens.astype(jnp.float32) + update).astype(jnp.bfloat16)


TOKEN_CHUNKS = 8
WEIGHT_CHUNKS = 16
GATED_CHUNKS = 4
ANY = pl.BlockSpec(memory_space=pl.ANY)


def remote(src, dst, send_sem, recv_sem, where):
    return pltpu.make_async_remote_copy(
        src_ref=src,
        dst_ref=dst,
        send_sem=send_sem,
        recv_sem=recv_sem,
        device_id=where,
        device_id_type=pl.DeviceIdType.MESH,
    )


def greet(devices):
    barrier = pltpu.get_barrier_semaphore()
    for where, present in devices:

        @pl.when(present)
        def _():
            pl.semaphore_signal(
                barrier, inc=1, device_id=where, device_id_type=pl.DeviceIdType.MESH
            )

    pl.semaphore_wait(
        barrier, sum(jnp.asarray(present).astype(jnp.int32) for _, present in devices)
    )


class Line:
    def __init__(self, view, count, chunks, send_sem, recv_sem, place):
        self.view, self.count, self.chunks = view, count, chunks
        self.send_sem, self.recv_sem, self.place = send_sem, recv_sem, place
        self.me = lax.axis_index("chan")

    def copy(self, way, step, chunk, src=None):
        step_to = 1 if way == 0 else -1
        owner = jnp.clip(self.me - step * step_to, 0, self.count - 1)
        target = jnp.clip(self.me + step_to, 0, self.count - 1)
        block = self.view(owner, chunk)
        return remote(
            block if src is None else src,
            block,
            self.send_sem.at[way, step, chunk],
            self.recv_sem.at[way, step, chunk],
            self.place(target),
        )

    def sends(self, way, step):
        if way == 0:
            return (self.me - step >= 0) & (self.me + 1 < self.count)
        return (self.me + step < self.count) & (self.me - 1 >= 0)

    def receives(self, way, step):
        if way == 0:
            return self.me - 1 - step >= 0
        return self.me + 1 + step < self.count

    def arrived(self, way, step, chunk):
        step_to = 1 if way == 0 else -1
        owner = jnp.clip(self.me - (step + 1) * step_to, 0, self.count - 1)
        block = self.view(owner, chunk)
        remote(
            block,
            block,
            self.send_sem.at[way, step, chunk],
            self.recv_sem.at[way, step, chunk],
            self.place(self.me),
        ).wait_recv()
        return owner


def gather_inputs_kernel(
    sizes,
    tokens,
    weights,
    taps,
    all_tokens,
    all_weights,
    all_taps,
    token_room,
    weight_room,
    tap_room,
    local_sem,
    line_send,
    line_recv,
    mate_send,
    mate_recv,
    x_send,
    x_recv,
    y_send,
    y_recv,
    f_send,
    f_recv,
):
    chan_count = sizes
    y, s, z = (lax.axis_index(name) for name in ("groups", "seq", "chan"))
    x, core = s // 2, s % 2
    mate = (y, s + 1 - 2 * core, z)
    across = lambda to: (y, (1 - x) * 2 + to, z)
    beside = (1 - y, s, z)
    rows, width = tokens.shape
    branches, depth, columns = weights.shape[0], weights.shape[1], weights.shape[2] // 2
    lags = taps.shape[2]
    half, half_lags = depth // 2, lags // 2

    greet(
        [
            (mate, True),
            (across(0), True),
            (across(1), True),
            (beside, True),
            ((y, s, jnp.minimum(z + 1, chan_count - 1)), z + 1 < chan_count),
            ((y, s, jnp.maximum(z - 1, 0)), z > 0),
        ]
    )

    token_rows = rows // TOKEN_CHUNKS
    weight_rows = half // WEIGHT_CHUNKS

    def token_view(owner, chunk):
        return all_tokens.at[
            pl.ds(core * rows + chunk * token_rows, token_rows), pl.ds(owner * width, width)
        ]

    line = Line(
        token_view, chan_count, TOKEN_CHUNKS, line_send, line_recv, lambda to: (y, s, to)
    )

    def weight_view(owner, part, chunk):
        return all_weights.at[pl.ds(owner * depth + part * half + chunk * weight_rows, weight_rows)]

    def tap_view(owner, part):
        return all_taps.at[pl.ds(owner * lags + part * half_lags, half_lags)]

    pending = []
    for chunk in range(TOKEN_CHUNKS):
        own = tokens.at[pl.ds(chunk * token_rows, token_rows)]
        for way in range(2):

            @pl.when(line.sends(way, 0))
            def _():
                line.copy(way, 0, chunk, own).start()

    for chunk in range(WEIGHT_CHUNKS):
        for to in range(2):
            view = weight_view(s, y, chunk)
            for b in range(branches):
                remote(
                    weights.at[
                        b,
                        pl.ds(y * half + chunk * weight_rows, weight_rows),
                        pl.ds(to * columns, columns),
                    ],
                    view.at[:, pl.ds(b * columns, columns)],
                    x_send.at[to, chunk],
                    x_recv.at[core, chunk],
                    across(to),
                ).start()
            pending.append(
                remote(view, view, x_send.at[to, chunk], x_recv.at[core, chunk], across(to))
            )
    for to in range(2):
        copy = remote(
            taps.at[to, 1 - x, pl.ds(y * half_lags, half_lags)],
            tap_view(s, y),
            f_send.at[to],
            f_recv.at[core],
            across(to),
        )
        copy.start()
        pending.append(copy)
    own_view = all_tokens.at[pl.ds(core * rows, rows), pl.ds(z * width, width)]
    mate_copies = [
        remote(tokens, own_view, mate_send.at[0], mate_recv.at[0], mate),
        remote(
            all_weights.at[pl.ds(s * depth, depth)],
            all_weights.at[pl.ds(s * depth, depth)],
            mate_send.at[1],
            mate_recv.at[1],
            mate,
        ),
        remote(
            taps.at[1 - core, x],
            all_taps.at[pl.ds(s * lags, lags)],
            mate_send.at[2],
            mate_recv.at[2],
            mate,
        ),
    ]
    for copy in (mate_copies[0], mate_copies[2]):
        copy.start()
    for b in range(branches):
        remote(
            weights.at[b, :, pl.ds((1 - core) * columns, columns)],
            all_weights.at[pl.ds(s * depth, depth), pl.ds(b * columns, columns)],
            mate_send.at[1],
            mate_recv.at[1],
            mate,
        ).start()
    ins = [
        pltpu.make_async_copy(tokens, token_room, local_sem.at[0]),
        pltpu.make_async_copy(taps.at[core, x], tap_room, local_sem.at[1]),
    ] + [
        pltpu.make_async_copy(
            weights.at[b, :, pl.ds(core * columns, columns)],
            weight_room.at[:, pl.ds(b * columns, columns)],
            local_sem.at[2 + b],
        )
        for b in range(branches)
    ]
    outs = [
        pltpu.make_async_copy(token_room, own_view, local_sem.at[5]),
        pltpu.make_async_copy(tap_room, all_taps.at[pl.ds(s * lags, lags)], local_sem.at[6]),
    ] + [
        pltpu.make_async_copy(
            weight_room.at[:, pl.ds(b * columns, columns)],
            all_weights.at[pl.ds(s * depth, depth), pl.ds(b * columns, columns)],
            local_sem.at[7 + b],
        )
        for b in range(branches)
    ]
    for copy in ins:
        copy.start()
    for first, second in zip(ins, outs):
        first.wait()
        second.start()

    def to_mate(way, step, chunk, owner):
        block = token_view(owner, chunk)
        index = 3 + (way * (chan_count - 1) + step) * TOKEN_CHUNKS + chunk
        return remote(block, block, mate_send.at[index], mate_recv.at[index], mate)

    steps = (chan_count - 1) * TOKEN_CHUNKS
    forwarded = 0
    for at in range(steps):
        step, chunk = divmod(at, TOKEN_CHUNKS)
        for way in range(2):

            @pl.when(line.receives(way, step))
            def _():
                owner = line.arrived(way, step, chunk)
                to_mate(way, step, chunk, owner).start()

            if step + 1 < chan_count - 1:

                @pl.when(line.receives(way, step) & line.sends(way, step + 1))
                def _():
                    line.copy(way, step + 1, chunk).start()

        while forwarded * steps < (at + 1) * WEIGHT_CHUNKS and forwarded < WEIGHT_CHUNKS:
            if (forwarded + 1) * steps > (at + 1) * WEIGHT_CHUNKS:
                break
            for origin in range(2):
                view = weight_view((1 - x) * 2 + origin, y, forwarded)
                remote(
                    view, view, x_send.at[origin, forwarded], x_recv.at[origin, forwarded], beside
                ).wait_recv()
                copy = remote(
                    view, view, y_send.at[origin, forwarded], y_recv.at[origin, forwarded], beside
                )
                copy.start()
                pending.append(copy)
            forwarded += 1
    for origin in range(2):
        view = tap_view((1 - x) * 2 + origin, y)
        remote(view, view, f_send.at[origin], f_recv.at[origin], beside).wait_recv()
        copy = remote(view, view, f_send.at[2 + origin], f_recv.at[2 + origin], beside)
        copy.start()
        pending.append(copy)

    for origin in range(2):
        owner = (1 - x) * 2 + origin
        for chunk in range(WEIGHT_CHUNKS):
            view = weight_view(owner, 1 - y, chunk)
            remote(
                view, view, y_send.at[origin, chunk], y_recv.at[origin, chunk], beside
            ).wait_recv()
        view = tap_view(owner, 1 - y)
        remote(view, view, f_send.at[2 + origin], f_recv.at[2 + origin], beside).wait_recv()
    for copy in outs:
        copy.wait()
    for copy in mate_copies:
        copy.wait_send()
    other_core = 1 - core
    mate_s = s + 1 - 2 * core
    for src, dst, index in (
        (tokens, all_tokens.at[pl.ds(other_core * rows, rows), pl.ds(z * width, width)], 0),
        (
            all_weights.at[pl.ds(mate_s * depth, depth)],
            all_weights.at[pl.ds(mate_s * depth, depth)],
            1,
        ),
        (taps.at[0, 0], all_taps.at[pl.ds(mate_s * lags, lags)], 2),
    ):
        remote(src, dst, mate_send.at[index], mate_recv.at[index], mate).wait_recv()
    for at in range(steps):
        step, chunk = divmod(at, TOKEN_CHUNKS)
        for way in range(2):

            @pl.when(line.sends(way, step))
            def _():
                line.copy(way, step, chunk).wait_send()

            @pl.when(line.receives(way, step))
            def _():
                sign = 1 if way == 0 else -1
                owner = jnp.clip(z - (step + 1) * sign, 0, chan_count - 1)
                to_mate(way, step, chunk, owner).wait_send()
                block = all_tokens.at[
                    pl.ds(other_core * rows + chunk * token_rows, token_rows),
                    pl.ds(owner * width, width),
                ]
                index = 3 + (way * (chan_count - 1) + step) * TOKEN_CHUNKS + chunk
                remote(block, block, mate_send.at[index], mate_recv.at[index], mate).wait_recv()

    for copy in pending:
        copy.wait_send()


def gather_inputs(tokens, weights, taps, chan_count):
    rows, width = tokens.shape
    branches, depth, both = weights.shape
    columns = branches * both // 2
    lags, share = taps.shape[2:]
    mate_count = 3 + 2 * (chan_count - 1) * TOKEN_CHUNKS
    dma = pltpu.SemaphoreType.DMA
    return pl.pallas_call(
        functools.partial(gather_inputs_kernel, chan_count),
        out_shape=(
            jax.ShapeDtypeStruct((2 * rows, chan_count * width), tokens.dtype),
            jax.ShapeDtypeStruct((4 * depth, columns), weights.dtype),
            jax.ShapeDtypeStruct((4 * lags, share), taps.dtype),
        ),
        in_specs=[ANY] * 3,
        out_specs=[ANY] * 3,
        scratch_shapes=[
            pltpu.VMEM((rows, width), tokens.dtype),
            pltpu.VMEM((depth, columns), weights.dtype),
            pltpu.VMEM((lags, share), taps.dtype),
            dma((10,)),
            dma((2, chan_count - 1, TOKEN_CHUNKS)),
            dma((2, chan_count - 1, TOKEN_CHUNKS)),
            dma((mate_count,)),
            dma((mate_count,)),
            dma((2, WEIGHT_CHUNKS)),
            dma((2, WEIGHT_CHUNKS)),
            dma((2, WEIGHT_CHUNKS)),
            dma((2, WEIGHT_CHUNKS)),
            dma((4,)),
            dma((4,)),
        ],
        compiler_params=pltpu.CompilerParams(
            collective_id=0, has_side_effects=True
        ),
        name="gather_inputs",
    )(tokens, weights, taps)


def fourier_tables(length):
    points = 2 * length
    first = 1 << ((points.bit_length() - 1) // 2)
    second = points // first
    kept = first // 2 + 1
    padded = -(-2 * kept // 8) * 8
    low = np.arange(kept)
    place = second * np.arange(first // 2)[None, :] + np.arange(second)[:, None]
    angle = (low[None, :, None] * place[:, None, :] % points) * (2 * np.pi / points)
    outer = np.zeros((second, padded, first // 2))
    outer[:, :kept] = np.cos(angle)
    outer[:, kept : 2 * kept] = -np.sin(angle)
    gain = np.where((low == 0) | (low == first // 2), 1.0, 2.0)[None, None, :] / points
    back = np.zeros((second, first // 2, padded))
    back[:, :, :kept] = np.cos(angle).transpose(0, 2, 1) * gain
    back[:, :, kept : 2 * kept] = -np.sin(angle).transpose(0, 2, 1) * gain
    inner = (np.arange(second)[:, None] * np.arange(second)[None, :] % second) * (
        2 * np.pi / second
    )
    cos, sin = np.cos(inner), np.sin(inner)
    ahead = np.block([[cos, sin], [-sin, cos]])
    behind = np.block([[cos, -sin], [sin, cos]])
    return first, second, kept, padded, [
        jnp.asarray(table, jnp.bfloat16) for table in (outer, ahead, behind, back)
    ]


def conv_phases(
    dims, signal, taps, skip, outer, ahead, behind, back, result, wide, spectra, total
):
    first, second, kept, padded = dims
    length, width = signal.shape
    reach = first // 2
    block = 64
    lanes = 128
    parts = width // lanes

    lanes = 128
    parts = width // lanes

    def ahead_outer():
        @pl.loop(0, length // block)
        def _(at):
            rows = pl.ds(pl.multiple_of(at * block, block), block)
            for part in range(parts):
                cols = pl.ds(part * lanes, lanes)
                wide[part, rows, :] = signal[rows, cols].astype(jnp.float32)
                wide[parts + part, rows, :] = taps[rows, cols].astype(jnp.float32)

        for part in range(parts):
            wide[parts + part, 0:1, :] = (
                wide[parts + part, 0:1, :] + skip[:, part * lanes : (part + 1) * lanes]
            )

        @pl.loop(0, second, unroll=4)
        def _(b):
            picked = jnp.concatenate(
                [wide.at[part][pl.ds(b, reach, stride=second), :] for part in range(2 * parts)],
                axis=1,
            ).astype(jnp.bfloat16)
            found = jnp.dot(outer[b], picked, preferred_element_type=jnp.float32)
            rows = pl.ds(pl.multiple_of(b * padded, 8), padded)
            for part in range(2 * parts):
                spectra[part, rows, :] = found[:, part * lanes : (part + 1) * lanes]

    def inner():
        def strided(start):
            return [
                spectra.at[part][pl.ds(start, second, stride=padded), :] for part in range(2 * parts)
            ]

        @pl.loop(0, kept, unroll=3)
        def _(k):
            real = jnp.concatenate(strided(k), axis=1)
            imag = jnp.concatenate(strided(k + kept), axis=1)
            both = jnp.concatenate([real, imag], axis=0).astype(jnp.bfloat16)
            freq = jnp.dot(ahead[...], both, preferred_element_type=jnp.float32)
            sr, si = freq[:second, :width], freq[second:, :width]
            hr, hi = freq[:second, width:], freq[second:, width:]
            product = jnp.concatenate([sr * hr - si * hi, sr * hi + si * hr], axis=0)
            inv = jnp.dot(
                behind[...], product.astype(jnp.bfloat16), preferred_element_type=jnp.float32
            )
            for part in range(parts):
                cols = slice(part * lanes, (part + 1) * lanes)
                spectra.at[part][pl.ds(k, second, stride=padded), :] = inv[:second, cols]
                spectra.at[part][pl.ds(k + kept, second, stride=padded), :] = inv[second:, cols]

    def back_outer():
        @pl.loop(0, second, unroll=4)
        def _(b):
            rows = pl.ds(pl.multiple_of(b * padded, 8), padded)
            filled = jnp.concatenate([spectra[part, rows, :] for part in range(parts)], axis=1)
            found = jnp.dot(back[b], filled.astype(jnp.bfloat16), preferred_element_type=jnp.float32)
            for part in range(parts):
                total.at[part][pl.ds(b, reach, stride=second), :] = found[
                    :, part * lanes : (part + 1) * lanes
                ]

        @pl.loop(0, length // block)
        def _(at):
            rows = pl.ds(pl.multiple_of(at * block, block), block)
            for part in range(parts):
                result[rows, part * lanes : (part + 1) * lanes] = total[part, rows, :].astype(
                    jnp.bfloat16
                )

    return ahead_outer, inner, back_outer


def long_conv_kernel(dims, *refs):
    for phase in conv_phases(dims, *refs):
        phase()


def long_conv(signal, taps, skip):
    length, width = signal.shape
    first, second, kept, padded, tables = fourier_tables(length)
    return pl.pallas_call(
        functools.partial(long_conv_kernel, (first, second, kept, padded)),
        out_shape=jax.ShapeDtypeStruct((length, width), jnp.bfloat16),
        scratch_shapes=[
            pltpu.VMEM((2 * width // 128, length, 128), jnp.float32),
            pltpu.VMEM((2 * width // 128, second * padded, 128), jnp.float32),
            pltpu.VMEM((width // 128, length, 128), jnp.float32),
        ],
        compiler_params=pltpu.CompilerParams(vmem_limit_bytes=56 * 1024 * 1024),
        cost_estimate=pl.CostEstimate(
            flops=2 * 64 * length * width * 40, bytes_accessed=6 * length * width, transcendentals=0
        ),
        name="long_conv",
    )(signal, taps, skip, *tables)


def mix_and_gather_kernel(
    dims,
    chan_count,
    gated,
    query,
    signal,
    taps,
    skip,
    outer,
    ahead,
    behind,
    back,
    full,
    wide,
    spectra,
    total,
    result,
    crossed,
    ready,
    room,
    local_sem,
    cross_sem,
    mate_send,
    mate_recv,
    line_send,
    line_recv,
):
    y, s, z = (lax.axis_index(name) for name in ("groups", "seq", "chan"))
    x, core = s // 2, s % 2
    mate = (y, s + 1 - 2 * core, z)
    across = (y, (1 - x) * 2 + core, z)
    _, rows, width = gated.shape
    half_chunks = GATED_CHUNKS // 2
    chunk_rows = rows // half_chunks
    greet(
        [
            (mate, True),
            (across, True),
            ((y, s, jnp.minimum(z + 1, chan_count - 1)), z + 1 < chan_count),
            ((y, s, jnp.maximum(z - 1, 0)), z > 0),
        ]
    )

    def column(part, owner, of):
        return ((owner * 2 + of) * 2 + part) * width

    lines = []
    for part in range(2):

        def view(owner, chunk, part=part):
            side, at = divmod(chunk, half_chunks)
            start = column(part, owner, core if side == 0 else 1 - core)
            return full.at[pl.ds(at * chunk_rows, chunk_rows), pl.ds(start, width)]

        lines.append(
            Line(
                view,
                chan_count,
                GATED_CHUNKS,
                line_send.at[part],
                line_recv.at[part],
                lambda to: (y, s, to),
            )
        )
    swaps = []

    def begin(part, source):
        line = lines[part]
        for at in range(half_chunks):
            piece = pl.ds(at * chunk_rows, chunk_rows)
            copy = remote(
                source.at[1 - core, piece],
                full.at[piece, pl.ds(column(part, z, core), width)],
                mate_send.at[part, at],
                mate_recv.at[part, at],
                mate,
            )
            copy.start()
            swaps.append(copy)
        for chunk in range(half_chunks):
            own = source.at[core, pl.ds(chunk * chunk_rows, chunk_rows)]
            for way in range(2):

                @pl.when(line.sends(way, 0))
                def _():
                    line.copy(way, 0, chunk, own).start()

        for at in range(half_chunks):
            block = full.at[
                pl.ds(at * chunk_rows, chunk_rows), pl.ds(column(part, z, 1 - core), width)
            ]
            remote(block, block, mate_send.at[part, at], mate_recv.at[part, at], mate).wait_recv()
            for way in range(2):

                @pl.when(line.sends(way, 0))
                def _():
                    line.copy(way, 0, half_chunks + at).start()

    def relay(part, step):
        line = lines[part]
        for chunk in range(GATED_CHUNKS):
            for way in range(2):

                @pl.when(line.receives(way, step))
                def _():
                    line.arrived(way, step, chunk)

                if step + 1 < chan_count - 1:

                    @pl.when(line.receives(way, step) & line.sends(way, step + 1))
                    def _():
                        line.copy(way, step + 1, chunk).start()

    ahead_outer, inner, back_outer = conv_phases(
        dims, signal, taps, skip, outer, ahead, behind, back, result, wide, spectra, total
    )
    take = pltpu.make_async_copy(gated.at[core], room, local_sem.at[0])
    take.start()
    begin(0, gated)
    take.wait()
    put = pltpu.make_async_copy(
        room, full.at[:, pl.ds(column(0, z, core), width)], local_sem.at[1]
    )
    put.start()
    ahead_outer()
    inner()
    relay(0, 0)
    back_outer()
    positions = 2 * rows
    cross = remote(
        result.at[pl.ds((1 - x) * positions, positions)],
        crossed,
        cross_sem.at[0],
        cross_sem.at[1],
        across,
    )
    cross.start()
    for step in range(1, chan_count - 2):
        relay(0, step)
    cross.wait()
    block = 64
    share = width // 2

    @pl.loop(0, positions // block)
    def _(at):
        start = pl.multiple_of(at * block, block)
        mine = result[pl.ds(pl.multiple_of(x * positions + start, block), block), :]
        other = crossed[pl.ds(start, block), :]
        low = jnp.where(x == 0, mine.astype(jnp.float32), other.astype(jnp.float32))
        high = jnp.where(x == 0, other.astype(jnp.float32), mine.astype(jnp.float32))
        asked = query[pl.ds(start, block), :].astype(jnp.float32)
        to = at // (rows // block)
        row = pl.ds(pl.multiple_of((at - to * (rows // block)) * block, block), block)
        ready[to, row, :share] = (asked[:, :share] * low).astype(jnp.bfloat16)
        ready[to, row, share:] = (asked[:, share:] * high).astype(jnp.bfloat16)

    begin(1, ready)
    last = pltpu.make_async_copy(
        ready.at[core], full.at[:, pl.ds(column(1, z, core), width)], local_sem.at[2]
    )
    last.start()
    relay(0, chan_count - 2)
    for step in range(chan_count - 1):
        relay(1, step)
    put.wait()
    last.wait()
    for copy in swaps:
        copy.wait_send()
    for line in lines:
        for step in range(chan_count - 1):
            for chunk in range(GATED_CHUNKS):
                for way in range(2):

                    @pl.when(line.sends(way, step))
                    def _():
                        line.copy(way, step, chunk).wait_send()


def mix_and_gather(gated, query, signal, taps, skip, chan_count):
    _, rows, width = gated.shape
    length, lanes = signal.shape
    first, second, kept, padded, tables = fourier_tables(length)
    dma = pltpu.SemaphoreType.DMA
    half_chunks = GATED_CHUNKS // 2
    vmem = pl.BlockSpec(memory_space=pltpu.VMEM)
    return pl.pallas_call(
        functools.partial(
            mix_and_gather_kernel, (first, second, kept, padded), chan_count
        ),
        out_shape=jax.ShapeDtypeStruct((rows, 4 * chan_count * width), gated.dtype),
        in_specs=[ANY] + [vmem] * 8,
        out_specs=ANY,
        scratch_shapes=[
            pltpu.VMEM((2 * lanes // 128, length, 128), jnp.float32),
            pltpu.VMEM((2 * lanes // 128, second * padded, 128), jnp.float32),
            pltpu.VMEM((lanes // 128, length, 128), jnp.float32),
            pltpu.VMEM((length, lanes), jnp.bfloat16),
            pltpu.VMEM((2 * rows, lanes), jnp.bfloat16),
            pltpu.VMEM((2, rows, width), jnp.bfloat16),
            pltpu.VMEM((rows, width), gated.dtype),
            dma((3,)),
            dma((2,)),
            dma((2, half_chunks)),
            dma((2, half_chunks)),
            dma((2, 2, chan_count - 1, GATED_CHUNKS)),
            dma((2, 2, chan_count - 1, GATED_CHUNKS)),
        ],
        compiler_params=pltpu.CompilerParams(
            collective_id=1, has_side_effects=True, vmem_limit_bytes=48 * 1024 * 1024
        ),
        name="mix_and_gather",
    )(gated, query, signal, taps, skip, *tables)


def chip_body(tokens, norm_gain, proj_weight, short_filter, long_filter, skip_gain, out_weight):
    seq_count, chan_count = lax.axis_size("seq"), lax.axis_size("chan")
    rows, width = tokens.shape
    depth, branches, local_chan = proj_weight.shape
    half = local_chan // 2
    share = half // 2
    lanes = share // 2
    s = lax.axis_index("seq")
    x, core = s // 2, s % 2
    weights = proj_weight.transpose(1, 0, 2)
    taps = (
        long_filter.astype(jnp.bfloat16)
        .reshape(2, 2, 2, lanes, rows)
        .transpose(0, 2, 4, 1, 3)
        .reshape(2, 2, rows, share)
    )
    whole, all_weights, all_taps = gather_inputs(tokens, weights, taps, chan_count)
    wide = whole.astype(jnp.float32)
    normed = (
        wide * lax.rsqrt(jnp.mean(wide * wide, axis=1, keepdims=True) + EPSILON) * norm_gain
    ).astype(jnp.bfloat16)
    projected = jnp.dot(normed, all_weights, preferred_element_type=jnp.float32).astype(
        jnp.bfloat16
    )
    rim = from_behind(projected[-(SHORT - 1) :], "seq", 2)
    short = lax.dynamic_slice_in_dim(short_filter, core * half, half, 2).reshape(
        SHORT, branches * half
    )
    extended = jnp.concatenate([rim, projected], axis=0).astype(jnp.float32)
    featured = jnp.zeros(projected.shape, jnp.float32)
    for tap in range(SHORT):
        start = SHORT - 1 - tap
        featured = featured + short[tap] * extended[start : start + projected.shape[0]]
    featured = featured.astype(jnp.bfloat16)
    middle = (
        featured[:, half : 2 * half].astype(jnp.float32)
        * featured[:, 2 * half :].astype(jnp.float32)
    ).astype(jnp.bfloat16)
    swap = [(at, (at + 2) % seq_count) for at in range(seq_count)]
    near = x == 0
    skip = lax.dynamic_slice_in_dim(skip_gain, core * half, half, 0).reshape(2, 2, lanes)
    skip = lax.dynamic_index_in_dim(skip, x, 1, keepdims=False)
    signals = []
    for part in range(2):
        pair = middle[:, part * share : (part + 1) * share]
        left, right = pair[:, :lanes], pair[:, lanes:]
        kept = jnp.where(near, left, right)
        other = lax.ppermute(jnp.where(near, right, left), "seq", swap)
        signals.append(
            jnp.concatenate([jnp.where(near, kept, other), jnp.where(near, other, kept)], axis=0)
        )
    longer = long_conv(signals[0], all_taps[:, :lanes], skip[:1])
    early, late = longer[: 2 * rows], longer[2 * rows :]
    kept = jnp.where(near, early, late)
    other = lax.ppermute(jnp.where(near, late, early), "seq", swap)
    longer = jnp.concatenate(
        [jnp.where(near, kept, other), jnp.where(near, other, kept)], axis=1
    )
    gated = (featured[:, :share].astype(jnp.float32) * longer.astype(jnp.float32)).astype(
        jnp.bfloat16
    )
    full_mix = mix_and_gather(
        gated.reshape(2, rows, share),
        featured[:, share:half],
        signals[1],
        all_taps[:, lanes:],
        skip[1:],
        chan_count,
    )
    update = jnp.dot(full_mix, out_weight, preferred_element_type=jnp.float32)
    return (tokens.astype(jnp.float32) + update).astype(jnp.bfloat16)


def select_body(mesh):
    if mesh.shape["seq"] == 4 and mesh.shape["groups"] == 2:
        return chip_body
    return body


def solution(mesh):
    placed = (
        P(("groups", "seq"), "chan"),
        P(),
        P("seq", None, "chan"),
        P(None, None, "chan"),
        P("chan", "seq"),
        P("chan"),
        P(None, "chan"),
    )
    return jax.shard_map(
        select_body(mesh), mesh=mesh, in_specs=placed, out_specs=P(("groups", "seq"), "chan"), check_vma=False
    )
```

```python
import functools
import math

import jax
import jax.numpy as jnp
import numpy as np
from jax import lax
from jax.experimental import pallas as pl
from jax.experimental.pallas import tpu as pltpu
from jax.sharding import PartitionSpec as P

SHORT = 3


EPSILON = 1e-06
HIGHEST = lax.Precision.HIGHEST


def from_behind(value, axis, steps):
    count = lax.axis_size(axis)
    initial, last = (max(0, -steps), min(count, count - steps))
    return lax.ppermute(value, axis, [(source, source + steps) for source in range(initial, last)])


def angle_table(row_count, col_count, period, sign):
    row_index = lax.iota(jnp.int32, row_count)[:, None]
    col_index = lax.iota(jnp.int32, col_count)[None, :]
    angles = (row_index * col_index % period).astype(jnp.float32) * (sign * 2.0 * math.pi / period)
    return (jnp.cos(angles), jnp.sin(angles))


def forward_spectrum(signal_rows, first, second):
    channels = signal_rows.shape[0]
    grid_rows = signal_rows.reshape(channels, first, second)
    cos_first, sin_first = angle_table(first, first, first, -1.0)
    part_re = jnp.einsum("cab,ak->ckb", grid_rows, cos_first, precision=HIGHEST)
    part_im = jnp.einsum("cab,ak->ckb", grid_rows, sin_first, precision=HIGHEST)
    twist_cos, twist_sin = angle_table(first, second, first * second, -1.0)
    part_re, part_im = (
        part_re * twist_cos - part_im * twist_sin,
        part_re * twist_sin + part_im * twist_cos,
    )
    cos_second, sin_second = angle_table(second, second, second, -1.0)
    spectrum_real = jnp.einsum("ckb,bm->ckm", part_re, cos_second, precision=HIGHEST) - jnp.einsum(
        "ckb,bm->ckm", part_im, sin_second, precision=HIGHEST
    )
    spec_im = jnp.einsum("ckb,bm->ckm", part_re, sin_second, precision=HIGHEST) + jnp.einsum(
        "ckb,bm->ckm", part_im, cos_second, precision=HIGHEST
    )
    return (spectrum_real, spec_im)


def inverse_spectrum(spectrum_real, spec_im, first, second):
    channels = spectrum_real.shape[0]
    cos_second, sin_second = angle_table(second, second, second, 1.0)
    part_re = jnp.einsum("ckm,bm->ckb", spectrum_real, cos_second, precision=HIGHEST) - jnp.einsum(
        "ckm,bm->ckb", spec_im, sin_second, precision=HIGHEST
    )
    part_im = jnp.einsum("ckm,bm->ckb", spectrum_real, sin_second, precision=HIGHEST) + jnp.einsum(
        "ckm,bm->ckb", spec_im, cos_second, precision=HIGHEST
    )
    twist_cos, twist_sin = angle_table(first, second, first * second, 1.0)
    part_re, part_im = (
        part_re * twist_cos - part_im * twist_sin,
        part_re * twist_sin + part_im * twist_cos,
    )
    cos_first, sin_first = angle_table(first, first, first, 1.0)
    result = jnp.einsum("ckb,ak->cab", part_re, cos_first, precision=HIGHEST) - jnp.einsum(
        "ckb,ak->cab", part_im, sin_first, precision=HIGHEST
    )
    return result.reshape(channels, first * second) / (first * second)


def spectral_conv(signal_rows, filter_rows):
    channels, length = signal_rows.shape
    padded_len = 2 * length
    log_len = padded_len.bit_length() - 1
    first = 1 << log_len // 2
    second = padded_len // first
    zeros_tail = jnp.zeros((channels, length), jnp.float32)
    sig_re, sig_im = forward_spectrum(
        jnp.concatenate([signal_rows, zeros_tail], axis=1), first, second
    )
    tap_re, tap_im = forward_spectrum(
        jnp.concatenate([filter_rows, zeros_tail], axis=1), first, second
    )
    prod_re = sig_re * tap_re - sig_im * tap_im
    prod_im = sig_re * tap_im + sig_im * tap_re
    return inverse_spectrum(prod_re, prod_im, first, second)[:, :length]


def short_filter_output(projected, rim_cells, kernel_coefficients):
    count = kernel_coefficients.shape[0]
    steps_len = projected.shape[2]
    extended = jnp.concatenate([rim_cells, projected], axis=2).astype(jnp.float32)
    total = jnp.zeros(projected.shape, jnp.float32)
    for tap in range(count):
        total = (
            total
            + kernel_coefficients[tap][:, :, None]
            * extended[:, :, count - 1 - tap : count - 1 - tap + steps_len]
        )
    return total.astype(jnp.bfloat16)


def hyena_mixer(keys_rows, values_rows, long_taps, skip_part):
    middle = keys_rows.astype(jnp.float32) * values_rows.astype(jnp.float32)
    return (spectral_conv(middle, long_taps) + skip_part[:, None] * middle).astype(jnp.bfloat16)


def body(tokens, norm_gain, proj_weight, short_filter, long_filter, skip_gain, out_weight):
    seq_count = lax.axis_size("seq")
    local_rows = tokens.shape[0]
    local_chan = proj_weight.shape[2]
    subset = local_chan // seq_count
    length = local_rows * seq_count
    offset = lax.axis_index("seq") * subset
    whole = lax.all_gather(tokens, "chan", axis=1, tiled=True)
    wide = whole.astype(jnp.float32)
    rescaled_signal = (
        wide * lax.rsqrt(jnp.mean(wide * wide, axis=1, keepdims=True) + EPSILON) * norm_gain
    ).astype(jnp.bfloat16)
    projected = lax.dot_general(
        lax.all_gather(proj_weight, "seq", axis=0, tiled=True),
        rescaled_signal,
        (((0,), (1,)), ((), ())),
        preferred_element_type=jnp.float32,
    ).astype(jnp.bfloat16)
    taps_grid = long_filter.reshape(1, seq_count, subset, local_rows)
    long_taps = lax.all_to_all(taps_grid, "seq", split_axis=1, concat_axis=3, tiled=True).reshape(
        subset, length
    )
    skip_part = lax.dynamic_slice_in_dim(skip_gain, offset, subset, 0)
    rim_cells = from_behind(projected[:, :, local_rows - (SHORT - 1) :], "seq", 1)
    featured = short_filter_output(projected, rim_cells, short_filter)
    pair_grid = featured[1:].reshape(2, seq_count, subset, local_rows)
    moved = lax.all_to_all(pair_grid, "seq", split_axis=1, concat_axis=3, tiled=True).reshape(
        2, subset, length
    )
    result = hyena_mixer(moved[0], moved[1], long_taps, skip_part)
    returned = lax.all_to_all(
        result.reshape(1, subset, length), "seq", split_axis=2, concat_axis=0, tiled=True
    )
    returned = returned.reshape(local_chan, local_rows)
    gated = (featured[0].astype(jnp.float32) * returned.astype(jnp.float32)).astype(jnp.bfloat16)
    full_mix = lax.all_gather(gated, "chan", axis=0, tiled=True)
    update = lax.dot_general(
        full_mix, out_weight, (((0,), (0,)), ((), ())), preferred_element_type=jnp.float32
    )
    return (tokens.astype(jnp.float32) + update).astype(jnp.bfloat16)


TOKEN_CHUNKS = 8
WEIGHT_CHUNKS = 16
GATED_CHUNKS = 4
ANY = pl.BlockSpec(memory_space=pl.ANY)


def remote(src, dst, send_sem, recv_sem, where):
    return pltpu.make_async_remote_copy(
        src_ref=src,
        dst_ref=dst,
        send_sem=send_sem,
        recv_sem=recv_sem,
        device_id=where,
        device_id_type=pl.DeviceIdType.MESH,
    )


def greet(devices):
    barrier = pltpu.get_barrier_semaphore()
    for where, present in devices:

        @pl.when(present)
        def _():
            pl.semaphore_signal(
                barrier, inc=1, device_id=where, device_id_type=pl.DeviceIdType.MESH
            )

    pl.semaphore_wait(
        barrier, sum(jnp.asarray(present).astype(jnp.int32) for _, present in devices)
    )


class Line:
    def __init__(self, view, count, chunks, send_sem, recv_sem, place):
        self.view, self.count, self.chunks = view, count, chunks
        self.send_sem, self.recv_sem, self.place = send_sem, recv_sem, place
        self.me = lax.axis_index("chan")

    def copy(self, way, step, chunk, src=None):
        step_to = 1 if way == 0 else -1
        owner = jnp.clip(self.me - step * step_to, 0, self.count - 1)
        target = jnp.clip(self.me + step_to, 0, self.count - 1)
        block = self.view(owner, chunk)
        return remote(
            block if src is None else src,
            block,
            self.send_sem.at[way, step, chunk],
            self.recv_sem.at[way, step, chunk],
            self.place(target),
        )

    def sends(self, way, step):
        if way == 0:
            return (self.me - step >= 0) & (self.me + 1 < self.count)
        return (self.me + step < self.count) & (self.me - 1 >= 0)

    def receives(self, way, step):
        if way == 0:
            return self.me - 1 - step >= 0
        return self.me + 1 + step < self.count

    def arrived(self, way, step, chunk):
        step_to = 1 if way == 0 else -1
        owner = jnp.clip(self.me - (step + 1) * step_to, 0, self.count - 1)
        block = self.view(owner, chunk)
        remote(
            block,
            block,
            self.send_sem.at[way, step, chunk],
            self.recv_sem.at[way, step, chunk],
            self.place(self.me),
        ).wait_recv()
        return owner


def gather_inputs_kernel(
    sizes,
    tokens,
    weights,
    taps,
    all_tokens,
    all_weights,
    all_taps,
    token_room,
    weight_room,
    tap_room,
    local_sem,
    line_send,
    line_recv,
    mate_send,
    mate_recv,
    x_send,
    x_recv,
    y_send,
    y_recv,
    f_send,
    f_recv,
):
    chan_count = sizes
    y, s, z = (lax.axis_index(name) for name in ("groups", "seq", "chan"))
    x, core = s // 2, s % 2
    mate = (y, s + 1 - 2 * core, z)
    across = lambda to: (y, (1 - x) * 2 + to, z)
    beside = (1 - y, s, z)
    rows, width = tokens.shape
    branches, depth, columns = weights.shape[0], weights.shape[1], weights.shape[2] // 2
    lags = taps.shape[2]
    half, half_lags = depth // 2, lags // 2

    greet(
        [
            (mate, True),
            (across(0), True),
            (across(1), True),
            (beside, True),
            ((y, s, jnp.minimum(z + 1, chan_count - 1)), z + 1 < chan_count),
            ((y, s, jnp.maximum(z - 1, 0)), z > 0),
        ]
    )

    token_rows = rows // TOKEN_CHUNKS
    weight_rows = half // WEIGHT_CHUNKS

    def token_view(owner, chunk):
        return all_tokens.at[
            pl.ds(core * rows + chunk * token_rows, token_rows), pl.ds(owner * width, width)
        ]

    line = Line(
        token_view, chan_count, TOKEN_CHUNKS, line_send, line_recv, lambda to: (y, s, to)
    )

    def weight_view(owner, part, chunk):
        return all_weights.at[pl.ds(owner * depth + part * half + chunk * weight_rows, weight_rows)]

    def tap_view(owner, part):
        return all_taps.at[pl.ds(owner * lags + part * half_lags, half_lags)]

    pending = []
    for chunk in range(TOKEN_CHUNKS):
        own = tokens.at[pl.ds(chunk * token_rows, token_rows)]
        for way in range(2):

            @pl.when(line.sends(way, 0))
            def _():
                line.copy(way, 0, chunk, own).start()

    for to in range(2):
        copy = remote(
            taps.at[to, 1 - x, pl.ds(y * half_lags, half_lags)],
            tap_view(s, y),
            f_send.at[to],
            f_recv.at[core],
            across(to),
        )
        copy.start()
        pending.append(copy)
    for chunk in range(WEIGHT_CHUNKS):
        for to in range(2):
            view = weight_view(s, y, chunk)
            for b in range(branches):
                remote(
                    weights.at[
                        b,
                        pl.ds(y * half + chunk * weight_rows, weight_rows),
                        pl.ds(to * columns, columns),
                    ],
                    view.at[:, pl.ds(b * columns, columns)],
                    x_send.at[to, chunk],
                    x_recv.at[core, chunk],
                    across(to),
                ).start()
            pending.append(
                remote(view, view, x_send.at[to, chunk], x_recv.at[core, chunk], across(to))
            )
    own_view = all_tokens.at[pl.ds(core * rows, rows), pl.ds(z * width, width)]
    mate_copies = [
        remote(tokens, own_view, mate_send.at[0], mate_recv.at[0], mate),
        remote(
            all_weights.at[pl.ds(s * depth, depth)],
            all_weights.at[pl.ds(s * depth, depth)],
            mate_send.at[1],
            mate_recv.at[1],
            mate,
        ),
        remote(
            taps.at[1 - core, x],
            all_taps.at[pl.ds(s * lags, lags)],
            mate_send.at[2],
            mate_recv.at[2],
            mate,
        ),
    ]
    for copy in (mate_copies[0], mate_copies[2]):
        copy.start()
    for b in range(branches):
        remote(
            weights.at[b, :, pl.ds((1 - core) * columns, columns)],
            all_weights.at[pl.ds(s * depth, depth), pl.ds(b * columns, columns)],
            mate_send.at[1],
            mate_recv.at[1],
            mate,
        ).start()
    ins = [
        pltpu.make_async_copy(tokens, token_room, local_sem.at[0]),
        pltpu.make_async_copy(taps.at[core, x], tap_room, local_sem.at[1]),
    ] + [
        pltpu.make_async_copy(
            weights.at[b, :, pl.ds(core * columns, columns)],
            weight_room.at[:, pl.ds(b * columns, columns)],
            local_sem.at[2 + b],
        )
        for b in range(branches)
    ]
    outs = [
        pltpu.make_async_copy(token_room, own_view, local_sem.at[5]),
        pltpu.make_async_copy(tap_room, all_taps.at[pl.ds(s * lags, lags)], local_sem.at[6]),
    ] + [
        pltpu.make_async_copy(
            weight_room.at[:, pl.ds(b * columns, columns)],
            all_weights.at[pl.ds(s * depth, depth), pl.ds(b * columns, columns)],
            local_sem.at[7 + b],
        )
        for b in range(branches)
    ]
    for copy in ins:
        copy.start()
    for first, second in zip(ins, outs):
        first.wait()
        second.start()

    def to_mate(way, step, chunk, owner):
        block = token_view(owner, chunk)
        index = 3 + (way * (chan_count - 1) + step) * TOKEN_CHUNKS + chunk
        return remote(block, block, mate_send.at[index], mate_recv.at[index], mate)

    for origin in range(2):
        view = tap_view((1 - x) * 2 + origin, y)
        remote(view, view, f_send.at[origin], f_recv.at[origin], beside).wait_recv()
        copy = remote(view, view, f_send.at[2 + origin], f_recv.at[2 + origin], beside)
        copy.start()
        pending.append(copy)

    steps = (chan_count - 1) * TOKEN_CHUNKS
    forwarded = 0
    for at in range(steps):
        step, chunk = divmod(at, TOKEN_CHUNKS)
        for way in range(2):

            @pl.when(line.receives(way, step))
            def _():
                owner = line.arrived(way, step, chunk)
                to_mate(way, step, chunk, owner).start()

            if step + 1 < chan_count - 1:

                @pl.when(line.receives(way, step) & line.sends(way, step + 1))
                def _():
                    line.copy(way, step + 1, chunk).start()

        while forwarded * steps < (at + 1) * WEIGHT_CHUNKS and forwarded < WEIGHT_CHUNKS:
            if (forwarded + 1) * steps > (at + 1) * WEIGHT_CHUNKS:
                break
            for origin in range(2):
                view = weight_view((1 - x) * 2 + origin, y, forwarded)
                remote(
                    view, view, x_send.at[origin, forwarded], x_recv.at[origin, forwarded], beside
                ).wait_recv()
                copy = remote(
                    view, view, y_send.at[origin, forwarded], y_recv.at[origin, forwarded], beside
                )
                copy.start()
                pending.append(copy)
            forwarded += 1
    for origin in range(2):
        owner = (1 - x) * 2 + origin
        for chunk in range(WEIGHT_CHUNKS):
            view = weight_view(owner, 1 - y, chunk)
            remote(
                view, view, y_send.at[origin, chunk], y_recv.at[origin, chunk], beside
            ).wait_recv()
        view = tap_view(owner, 1 - y)
        remote(view, view, f_send.at[2 + origin], f_recv.at[2 + origin], beside).wait_recv()
    for copy in outs:
        copy.wait()
    for copy in mate_copies:
        copy.wait_send()
    other_core = 1 - core
    mate_s = s + 1 - 2 * core
    for src, dst, index in (
        (tokens, all_tokens.at[pl.ds(other_core * rows, rows), pl.ds(z * width, width)], 0),
        (
            all_weights.at[pl.ds(mate_s * depth, depth)],
            all_weights.at[pl.ds(mate_s * depth, depth)],
            1,
        ),
        (taps.at[0, 0], all_taps.at[pl.ds(mate_s * lags, lags)], 2),
    ):
        remote(src, dst, mate_send.at[index], mate_recv.at[index], mate).wait_recv()
    for at in range(steps):
        step, chunk = divmod(at, TOKEN_CHUNKS)
        for way in range(2):

            @pl.when(line.sends(way, step))
            def _():
                line.copy(way, step, chunk).wait_send()

            @pl.when(line.receives(way, step))
            def _():
                sign = 1 if way == 0 else -1
                owner = jnp.clip(z - (step + 1) * sign, 0, chan_count - 1)
                to_mate(way, step, chunk, owner).wait_send()
                block = all_tokens.at[
                    pl.ds(other_core * rows + chunk * token_rows, token_rows),
                    pl.ds(owner * width, width),
                ]
                index = 3 + (way * (chan_count - 1) + step) * TOKEN_CHUNKS + chunk
                remote(block, block, mate_send.at[index], mate_recv.at[index], mate).wait_recv()

    for copy in pending:
        copy.wait_send()


def gather_inputs(tokens, weights, taps, chan_count):
    rows, width = tokens.shape
    branches, depth, both = weights.shape
    columns = branches * both // 2
    lags, share = taps.shape[2:]
    mate_count = 3 + 2 * (chan_count - 1) * TOKEN_CHUNKS
    dma = pltpu.SemaphoreType.DMA
    return pl.pallas_call(
        functools.partial(gather_inputs_kernel, chan_count),
        out_shape=(
            jax.ShapeDtypeStruct((2 * rows, chan_count * width), tokens.dtype),
            jax.ShapeDtypeStruct((4 * depth, columns), weights.dtype),
            jax.ShapeDtypeStruct((4 * lags, share), taps.dtype),
        ),
        in_specs=[ANY] * 3,
        out_specs=[ANY] * 3,
        scratch_shapes=[
            pltpu.VMEM((rows, width), tokens.dtype),
            pltpu.VMEM((depth, columns), weights.dtype),
            pltpu.VMEM((lags, share), taps.dtype),
            dma((10,)),
            dma((2, chan_count - 1, TOKEN_CHUNKS)),
            dma((2, chan_count - 1, TOKEN_CHUNKS)),
            dma((mate_count,)),
            dma((mate_count,)),
            dma((2, WEIGHT_CHUNKS)),
            dma((2, WEIGHT_CHUNKS)),
            dma((2, WEIGHT_CHUNKS)),
            dma((2, WEIGHT_CHUNKS)),
            dma((4,)),
            dma((4,)),
        ],
        compiler_params=pltpu.CompilerParams(
            collective_id=0, has_side_effects=True
        ),
        name="gather_inputs",
    )(tokens, weights, taps)


def fourier_tables(length):
    points = 2 * length
    first = 1 << ((points.bit_length() - 1) // 2)
    second = points // first
    kept = first // 2 + 1
    padded = -(-2 * kept // 8) * 8
    low = np.arange(kept)
    place = second * np.arange(first // 2)[None, :] + np.arange(second)[:, None]
    angle = (low[None, :, None] * place[:, None, :] % points) * (2 * np.pi / points)
    outer = np.zeros((second, padded, first // 2))
    outer[:, :kept] = np.cos(angle)
    outer[:, kept : 2 * kept] = -np.sin(angle)
    gain = np.where((low == 0) | (low == first // 2), 1.0, 2.0)[None, None, :] / points
    back = np.zeros((second, first // 2, padded))
    back[:, :, :kept] = np.cos(angle).transpose(0, 2, 1) * gain
    back[:, :, kept : 2 * kept] = -np.sin(angle).transpose(0, 2, 1) * gain
    inner = (np.arange(second)[:, None] * np.arange(second)[None, :] % second) * (
        2 * np.pi / second
    )
    cos, sin = np.cos(inner), np.sin(inner)
    ahead = np.block([[cos, sin], [-sin, cos]])
    behind = np.block([[cos, -sin], [sin, cos]])
    return first, second, kept, padded, [
        jnp.asarray(table, jnp.bfloat16) for table in (outer, ahead, behind, back)
    ]


def conv_phases(
    dims, signal, taps, skip, outer, ahead, behind, back, result, wide, spectra, total
):
    first, second, kept, padded = dims
    length, width = signal.shape
    reach = first // 2
    block = 64
    lanes = 128
    parts = width // lanes

    lanes = 128
    parts = width // lanes

    def ahead_outer():
        @pl.loop(0, length // block)
        def _(at):
            rows = pl.ds(pl.multiple_of(at * block, block), block)
            for part in range(parts):
                cols = pl.ds(part * lanes, lanes)
                wide[part, rows, :] = signal[rows, cols].astype(jnp.float32)
                wide[parts + part, rows, :] = taps[rows, cols].astype(jnp.float32)

        for part in range(parts):
            wide[parts + part, 0:1, :] = (
                wide[parts + part, 0:1, :] + skip[:, part * lanes : (part + 1) * lanes]
            )

        @pl.loop(0, second, unroll=4)
        def _(b):
            picked = jnp.concatenate(
                [wide.at[part][pl.ds(b, reach, stride=second), :] for part in range(2 * parts)],
                axis=1,
            ).astype(jnp.bfloat16)
            found = jnp.dot(outer[b], picked, preferred_element_type=jnp.float32)
            rows = pl.ds(pl.multiple_of(b * padded, 8), padded)
            for part in range(2 * parts):
                spectra[part, rows, :] = found[:, part * lanes : (part + 1) * lanes]

    def inner():
        def strided(start):
            return [
                spectra.at[part][pl.ds(start, second, stride=padded), :] for part in range(2 * parts)
            ]

        @pl.loop(0, kept, unroll=3)
        def _(k):
            real = jnp.concatenate(strided(k), axis=1)
            imag = jnp.concatenate(strided(k + kept), axis=1)
            both = jnp.concatenate([real, imag], axis=0).astype(jnp.bfloat16)
            freq = jnp.dot(ahead[...], both, preferred_element_type=jnp.float32)
            sr, si = freq[:second, :width], freq[second:, :width]
            hr, hi = freq[:second, width:], freq[second:, width:]
            product = jnp.concatenate([sr * hr - si * hi, sr * hi + si * hr], axis=0)
            inv = jnp.dot(
                behind[...], product.astype(jnp.bfloat16), preferred_element_type=jnp.float32
            )
            for part in range(parts):
                cols = slice(part * lanes, (part + 1) * lanes)
                spectra.at[part][pl.ds(k, second, stride=padded), :] = inv[:second, cols]
                spectra.at[part][pl.ds(k + kept, second, stride=padded), :] = inv[second:, cols]

    def back_outer():
        @pl.loop(0, second, unroll=4)
        def _(b):
            rows = pl.ds(pl.multiple_of(b * padded, 8), padded)
            filled = jnp.concatenate([spectra[part, rows, :] for part in range(parts)], axis=1)
            found = jnp.dot(back[b], filled.astype(jnp.bfloat16), preferred_element_type=jnp.float32)
            for part in range(parts):
                total.at[part][pl.ds(b, reach, stride=second), :] = found[
                    :, part * lanes : (part + 1) * lanes
                ]

        @pl.loop(0, length // block)
        def _(at):
            rows = pl.ds(pl.multiple_of(at * block, block), block)
            for part in range(parts):
                result[rows, part * lanes : (part + 1) * lanes] = total[part, rows, :].astype(
                    jnp.bfloat16
                )

    return ahead_outer, inner, back_outer


def long_conv_kernel(dims, *refs):
    for phase in conv_phases(dims, *refs):
        phase()


def long_conv(signal, taps, skip):
    length, width = signal.shape
    first, second, kept, padded, tables = fourier_tables(length)
    return pl.pallas_call(
        functools.partial(long_conv_kernel, (first, second, kept, padded)),
        out_shape=jax.ShapeDtypeStruct((length, width), jnp.bfloat16),
        scratch_shapes=[
            pltpu.VMEM((2 * width // 128, length, 128), jnp.float32),
            pltpu.VMEM((2 * width // 128, second * padded, 128), jnp.float32),
            pltpu.VMEM((width // 128, length, 128), jnp.float32),
        ],
        compiler_params=pltpu.CompilerParams(vmem_limit_bytes=56 * 1024 * 1024),
        cost_estimate=pl.CostEstimate(
            flops=2 * 64 * length * width * 40, bytes_accessed=6 * length * width, transcendentals=0
        ),
        name="long_conv",
    )(signal, taps, skip, *tables)


def mix_and_gather_kernel(
    dims,
    chan_count,
    gated,
    query,
    signal,
    taps,
    skip,
    outer,
    ahead,
    behind,
    back,
    full,
    wide,
    spectra,
    total,
    result,
    crossed,
    ready,
    room,
    local_sem,
    cross_sem,
    mate_send,
    mate_recv,
    line_send,
    line_recv,
):
    y, s, z = (lax.axis_index(name) for name in ("groups", "seq", "chan"))
    x, core = s // 2, s % 2
    mate = (y, s + 1 - 2 * core, z)
    across = (y, (1 - x) * 2 + core, z)
    _, rows, width = gated.shape
    half_chunks = GATED_CHUNKS // 2
    chunk_rows = rows // half_chunks
    greet(
        [
            (mate, True),
            (across, True),
            ((y, s, jnp.minimum(z + 1, chan_count - 1)), z + 1 < chan_count),
            ((y, s, jnp.maximum(z - 1, 0)), z > 0),
        ]
    )

    def column(part, owner, of):
        return ((owner * 2 + of) * 2 + part) * width

    lines = []
    for part in range(2):

        def view(owner, chunk, part=part):
            side, at = divmod(chunk, half_chunks)
            start = column(part, owner, core if side == 0 else 1 - core)
            return full.at[pl.ds(at * chunk_rows, chunk_rows), pl.ds(start, width)]

        lines.append(
            Line(
                view,
                chan_count,
                GATED_CHUNKS,
                line_send.at[part],
                line_recv.at[part],
                lambda to: (y, s, to),
            )
        )
    swaps = []

    def begin(part, source):
        line = lines[part]
        for at in range(half_chunks):
            piece = pl.ds(at * chunk_rows, chunk_rows)
            copy = remote(
                source.at[1 - core, piece],
                full.at[piece, pl.ds(column(part, z, core), width)],
                mate_send.at[part, at],
                mate_recv.at[part, at],
                mate,
            )
            copy.start()
            swaps.append(copy)
        for chunk in range(half_chunks):
            own = source.at[core, pl.ds(chunk * chunk_rows, chunk_rows)]
            for way in range(2):

                @pl.when(line.sends(way, 0))
                def _():
                    line.copy(way, 0, chunk, own).start()

        for at in range(half_chunks):
            block = full.at[
                pl.ds(at * chunk_rows, chunk_rows), pl.ds(column(part, z, 1 - core), width)
            ]
            remote(block, block, mate_send.at[part, at], mate_recv.at[part, at], mate).wait_recv()
            for way in range(2):

                @pl.when(line.sends(way, 0))
                def _():
                    line.copy(way, 0, half_chunks + at).start()

    def relay(part, step):
        line = lines[part]
        for chunk in range(GATED_CHUNKS):
            for way in range(2):

                @pl.when(line.receives(way, step))
                def _():
                    line.arrived(way, step, chunk)

                if step + 1 < chan_count - 1:

                    @pl.when(line.receives(way, step) & line.sends(way, step + 1))
                    def _():
                        line.copy(way, step + 1, chunk).start()

    ahead_outer, inner, back_outer = conv_phases(
        dims, signal, taps, skip, outer, ahead, behind, back, result, wide, spectra, total
    )
    take = pltpu.make_async_copy(gated.at[core], room, local_sem.at[0])
    take.start()
    begin(0, gated)
    take.wait()
    put = pltpu.make_async_copy(
        room, full.at[:, pl.ds(column(0, z, core), width)], local_sem.at[1]
    )
    put.start()
    ahead_outer()
    inner()
    relay(0, 0)
    back_outer()
    positions = 2 * rows
    cross = remote(
        result.at[pl.ds((1 - x) * positions, positions)],
        crossed,
        cross_sem.at[0],
        cross_sem.at[1],
        across,
    )
    cross.start()
    for step in range(1, chan_count - 2):
        relay(0, step)
    cross.wait()
    block = 64
    share = width // 2

    @pl.loop(0, positions // block)
    def _(at):
        start = pl.multiple_of(at * block, block)
        mine = result[pl.ds(pl.multiple_of(x * positions + start, block), block), :]
        other = crossed[pl.ds(start, block), :]
        low = jnp.where(x == 0, mine.astype(jnp.float32), other.astype(jnp.float32))
        high = jnp.where(x == 0, other.astype(jnp.float32), mine.astype(jnp.float32))
        asked = query[pl.ds(start, block), :].astype(jnp.float32)
        to = at // (rows // block)
        row = pl.ds(pl.multiple_of((at - to * (rows // block)) * block, block), block)
        ready[to, row, :share] = (asked[:, :share] * low).astype(jnp.bfloat16)
        ready[to, row, share:] = (asked[:, share:] * high).astype(jnp.bfloat16)

    begin(1, ready)
    last = pltpu.make_async_copy(
        ready.at[core], full.at[:, pl.ds(column(1, z, core), width)], local_sem.at[2]
    )
    last.start()
    relay(0, chan_count - 2)
    for step in range(chan_count - 1):
        relay(1, step)
    put.wait()
    last.wait()
    for copy in swaps:
        copy.wait_send()
    for line in lines:
        for step in range(chan_count - 1):
            for chunk in range(GATED_CHUNKS):
                for way in range(2):

                    @pl.when(line.sends(way, step))
                    def _():
                        line.copy(way, step, chunk).wait_send()


def mix_and_gather(gated, query, signal, taps, skip, chan_count):
    _, rows, width = gated.shape
    length, lanes = signal.shape
    first, second, kept, padded, tables = fourier_tables(length)
    dma = pltpu.SemaphoreType.DMA
    half_chunks = GATED_CHUNKS // 2
    vmem = pl.BlockSpec(memory_space=pltpu.VMEM)
    return pl.pallas_call(
        functools.partial(
            mix_and_gather_kernel, (first, second, kept, padded), chan_count
        ),
        out_shape=jax.ShapeDtypeStruct((rows, 4 * chan_count * width), gated.dtype),
        in_specs=[ANY] + [vmem] * 8,
        out_specs=ANY,
        scratch_shapes=[
            pltpu.VMEM((2 * lanes // 128, length, 128), jnp.float32),
            pltpu.VMEM((2 * lanes // 128, second * padded, 128), jnp.float32),
            pltpu.VMEM((lanes // 128, length, 128), jnp.float32),
            pltpu.VMEM((length, lanes), jnp.bfloat16),
            pltpu.VMEM((2 * rows, lanes), jnp.bfloat16),
            pltpu.VMEM((2, rows, width), jnp.bfloat16),
            pltpu.VMEM((rows, width), gated.dtype),
            dma((3,)),
            dma((2,)),
            dma((2, half_chunks)),
            dma((2, half_chunks)),
            dma((2, 2, chan_count - 1, GATED_CHUNKS)),
            dma((2, 2, chan_count - 1, GATED_CHUNKS)),
        ],
        compiler_params=pltpu.CompilerParams(
            collective_id=1, has_side_effects=True, vmem_limit_bytes=48 * 1024 * 1024
        ),
        name="mix_and_gather",
    )(gated, query, signal, taps, skip, *tables)


def chip_body(tokens, norm_gain, proj_weight, short_filter, long_filter, skip_gain, out_weight):
    seq_count, chan_count = lax.axis_size("seq"), lax.axis_size("chan")
    rows, width = tokens.shape
    depth, branches, local_chan = proj_weight.shape
    half = local_chan // 2
    share = half // 2
    lanes = share // 2
    s = lax.axis_index("seq")
    x, core = s // 2, s % 2
    weights = proj_weight.transpose(1, 0, 2)
    taps = (
        long_filter.astype(jnp.bfloat16)
        .reshape(2, 2, 2, lanes, rows)
        .transpose(0, 2, 4, 1, 3)
        .reshape(2, 2, rows, share)
    )
    whole, all_weights, all_taps = gather_inputs(tokens, weights, taps, chan_count)
    wide = whole.astype(jnp.float32)
    normed = (
        wide * lax.rsqrt(jnp.mean(wide * wide, axis=1, keepdims=True) + EPSILON) * norm_gain
    ).astype(jnp.bfloat16)
    projected = jnp.dot(normed, all_weights, preferred_element_type=jnp.float32).astype(
        jnp.bfloat16
    )
    rim = from_behind(projected[-(SHORT - 1) :], "seq", 2)
    short = lax.dynamic_slice_in_dim(short_filter, core * half, half, 2).reshape(
        SHORT, branches * half
    )
    extended = jnp.concatenate([rim, projected], axis=0).astype(jnp.float32)
    featured = jnp.zeros(projected.shape, jnp.float32)
    for tap in range(SHORT):
        start = SHORT - 1 - tap
        featured = featured + short[tap] * extended[start : start + projected.shape[0]]
    featured = featured.astype(jnp.bfloat16)
    middle = (
        featured[:, half : 2 * half].astype(jnp.float32)
        * featured[:, 2 * half :].astype(jnp.float32)
    ).astype(jnp.bfloat16)
    swap = [(at, (at + 2) % seq_count) for at in range(seq_count)]
    near = x == 0
    skip = lax.dynamic_slice_in_dim(skip_gain, core * half, half, 0).reshape(2, 2, lanes)
    skip = lax.dynamic_index_in_dim(skip, x, 1, keepdims=False)
    def joined(pair, other):
        left, right = pair[:, :lanes], pair[:, lanes:]
        kept = jnp.where(near, left, right)
        return jnp.concatenate(
            [jnp.where(near, kept, other), jnp.where(near, other, kept)], axis=0
        )

    pairs = [middle[:, :share], middle[:, share:]]
    others = [
        lax.ppermute(jnp.where(near, pair[:, lanes:], pair[:, :lanes]), "seq", swap)
        for pair in pairs
    ]
    longer = long_conv(joined(pairs[0], others[0]), all_taps[:, :lanes], skip[:1])
    longer, later = lax.optimization_barrier((longer, others[1]))
    signal = joined(pairs[1], later)
    early, late = longer[: 2 * rows], longer[2 * rows :]
    kept = jnp.where(near, early, late)
    other = lax.ppermute(jnp.where(near, late, early), "seq", swap)
    longer = jnp.concatenate(
        [jnp.where(near, kept, other), jnp.where(near, other, kept)], axis=1
    )
    gated = (featured[:, :share].astype(jnp.float32) * longer.astype(jnp.float32)).astype(
        jnp.bfloat16
    )
    full_mix = mix_and_gather(
        gated.reshape(2, rows, share),
        featured[:, share:half],
        signal,
        all_taps[:, lanes:],
        skip[1:],
        chan_count,
    )
    update = jnp.dot(full_mix, out_weight, preferred_element_type=jnp.float32)
    return (tokens.astype(jnp.float32) + update).astype(jnp.bfloat16)


def select_body(mesh):
    if mesh.shape["seq"] == 4 and mesh.shape["groups"] == 2:
        return chip_body
    return body


def solution(mesh):
    placed = (
        P(("groups", "seq"), "chan"),
        P(),
        P("seq", None, "chan"),
        P(None, None, "chan"),
        P("chan", "seq"),
        P("chan"),
        P(None, "chan"),
    )
    return jax.shard_map(
        select_body(mesh), mesh=mesh, in_specs=placed, out_specs=P(("groups", "seq"), "chan"), check_vma=False
    )
```
